128 devices in a mesh: frame: 16 (over x, y), pack: 8 (over z, core).
Axes of the slice: x: 4, y: 4, z: 4, core: 2. Of those that a mesh axis runs over, the one named last changes fastest.
Arguments:
- inputs: bfloat16 [16, 4096, 2240], P('frame', 'pack'), may hold values from -9 to 9
- weight: bfloat16 [2240, 3360], replicated, may hold values from -0.125 to 0.125
- clip_of_row: int32 [16, 4096], P('frame', 'pack'), may hold values from 0 to 1, as said below
- out_grad: bfloat16 [16, 4096, 1120], P('frame', 'pack'), may hold values from -6 to 6
Outputs:
- attention_out: bfloat16 [16, 4096, 1120], P('frame', 'pack')
- input_grad: bfloat16 [16, 4096, 2240], P('frame', 'pack')
The draws below stay inside these ranges and needn't reach their ends.
Inputs may be any that keep to these rules, and one draw needn't show every extreme that they name: `clip_of_row`: each device holds at most 384 rows of one clip, hence at least 128 rows of each; some device holds exactly 384 rows of clip 0 and another exactly 384 rows of clip 1; the number of rows of a clip on a device is the same for every frame index; rows of a device are in no particular order.
All inputs are finite; a program needn't handle non-finite values.
Results may differ from the reference program's by a relative error of at most 0.034.
Values may be sent and summed in bfloat16 or wider, within the bound.
A program may use at most 128 MiB of HBM per device.

```python
import jax
import jax.numpy as jnp
from jax import lax

D = 2240
HEADS = 10
HEAD = 112
TOK_DEV = 512
CLIPS = 2
HD = 1120
CAP = 384
FRAMES = 16
ROWS = 4096
N_PACK = 8


def packing_rows(key):
    base_key = jax.random.fold_in(key, 17)
    low_count = TOK_DEV - CAP
    first_counts = jax.random.randint(jax.random.fold_in(base_key, 2), (N_PACK,), low_count, CAP + 1).astype(jnp.int32)
    device_order = jax.random.permutation(jax.random.fold_in(base_key, 1), N_PACK).astype(jnp.int32)
    device_ids = jnp.arange(N_PACK, dtype=jnp.int32)
    first_counts = jnp.where(device_ids == device_order[0], CAP, first_counts)
    first_counts = jnp.where(device_ids == device_order[1], low_count, first_counts)
    positions = jnp.arange(TOK_DEV, dtype=jnp.int32)
    sorted_labels = (positions[None, :] >= first_counts[:, None]).astype(jnp.int32)

    def shuffle_one(frame_idx, pack_idx):
        shuffle_key = jax.random.fold_in(jax.random.fold_in(base_key, 100 + frame_idx), pack_idx)
        shuffle = jax.random.permutation(shuffle_key, TOK_DEV)
        return sorted_labels[pack_idx][shuffle]
    frame_ids = jnp.arange(FRAMES, dtype=jnp.int32)
    labels = jax.vmap(lambda frame_idx: jax.vmap(lambda pack_idx: shuffle_one(frame_idx, pack_idx))(device_ids))(frame_ids)
    return labels.astype(jnp.int32)


def draw_clip_of_row(key, part):
    return packing_rows(key).reshape(FRAMES, N_PACK * TOK_DEV)


def draw_inputs(key, part):
    labels = packing_rows(key)
    offset_table = jnp.clip(jax.random.normal(jax.random.fold_in(key, 29), (FRAMES, CLIPS, D), jnp.float32), -4.0, 4.0)
    offsets = jax.vmap(lambda table_rows, label_rows: table_rows[label_rows])(offset_table, labels)
    jitter_key = jax.random.fold_in(key, 23)
    draw_shape = (FRAMES, N_PACK, TOK_DEV, D)
    jitter_values = jnp.clip(jax.random.normal(jitter_key, draw_shape, jnp.float32), -4.0, 4.0)
    values = offsets + jitter_values
    return values.reshape(FRAMES, N_PACK * TOK_DEV, D).astype(jnp.bfloat16)


def shard_levels(own_key, dims, cuts, least, high):
    def one(axis_at, blocks):
        steps = jax.random.uniform(jax.random.fold_in(jax.random.fold_in(own_key, 6), axis_at), (blocks,), jnp.float32, least / len(cuts), high / len(cuts))
        return jnp.repeat(jnp.exp(steps), dims[axis_at] // blocks).reshape((-1,) + (1,) * (len(dims) - axis_at - 1))

    factor_of = one(*cuts[0])
    for cut in cuts[1:]:
        factor_of = factor_of * one(*cut)
    return factor_of


def bell_draw(key, shape, scale, reach, split=(), kind=jnp.bfloat16):
    values = scale * jax.random.normal(key, shape, jnp.float32)
    if split:
        values = values * shard_levels(key, shape, split, -0.22, 0.18)
    return jnp.clip(values, -reach, reach).astype(kind)


def setup_inputs(seed: int = 0) -> dict:
    key_list = jax.random.split(jax.random.key(seed), 5)
    inputs = draw_inputs(jax.random.fold_in(key_list[4], 71), 0)
    weight = bell_draw(key_list[1], (D, 3 * HD), D ** -0.5, 0.125)
    clip_of_row = draw_clip_of_row(jax.random.fold_in(key_list[4], 71), 0)
    out_grad = bell_draw(key_list[3], (FRAMES, ROWS, HD), 1.0, 6.0, ((0, 16), (1, 8)))
    return {"inputs": inputs, "weight": weight, "clip_of_row": clip_of_row, "out_grad": out_grad}


EPS = 1e-6


def slot_places(labels):
    onehot = (labels[:, None] == jnp.arange(CLIPS, dtype=jnp.int32)[None, :]).astype(jnp.int32)
    rank_in_clip = jnp.sum((jnp.cumsum(onehot, axis=0) - 1) * onehot, axis=1)
    return (labels * (N_PACK * CAP) + rank_in_clip).astype(jnp.int32)


def place_rows(values, places):
    return jnp.zeros((CLIPS * N_PACK * CAP, values.shape[1]), values.dtype).at[places].set(values)


def take_rows(values, places):
    return values[places]


def block_terms(feat_block):
    key_part = feat_block[:, :, 1].astype(jnp.float32)
    value_part = feat_block[:, :, 2].astype(jnp.float32)
    return jnp.einsum('cshd,cshe->chde', key_part, value_part), jnp.sum(key_part, axis=1)


def query_terms(operands):
    feat_block, state_low, norm_low, cotangent = operands
    query_part = feat_block[:, :, 0].astype(jnp.float32)
    numerator = jnp.einsum('cshd,chde->cshe', query_part, state_low.astype(jnp.float32))
    denominator = jnp.sum(query_part * norm_low.astype(jnp.float32)[:, None], axis=-1) + EPS
    attended = numerator / denominator[..., None]
    cotangent = cotangent.astype(jnp.float32)
    numer_grad = (cotangent / denominator[..., None]).astype(jnp.bfloat16)
    denom_grad = -jnp.sum(cotangent * attended, axis=-1) / denominator
    grad_block = jnp.einsum('cshd,cshe->chde', query_part, numer_grad.astype(jnp.float32))
    dnorm_block = jnp.sum(denom_grad[..., None] * query_part, axis=1)
    return attended.astype(jnp.bfloat16), numer_grad, denom_grad, grad_block, dnorm_block


def back_terms(operands):
    feat_block, numer_grad, denom_grad, state_low, norm_low, grad_low, dnorm_low = operands
    query_part = feat_block[:, :, 0].astype(jnp.float32)
    key_part = feat_block[:, :, 1].astype(jnp.float32)
    value_part = feat_block[:, :, 2].astype(jnp.float32)
    query_grad = jnp.einsum('cshe,chde->cshd', numer_grad.astype(jnp.float32), state_low.astype(jnp.float32))
    query_grad = query_grad + denom_grad[..., None] * norm_low.astype(jnp.float32)[:, None]
    query_grad = jnp.where(query_part > 0, query_grad, 0.0)
    key_grad = jnp.einsum('cshe,chde->cshd', value_part, grad_low.astype(jnp.float32)) + dnorm_low.astype(jnp.float32)[:, None]
    key_grad = jnp.where(key_part > 0, key_grad, 0.0)
    value_grad = jnp.einsum('cshd,chde->cshe', key_part, grad_low.astype(jnp.float32))
    return jnp.stack([query_grad, key_grad, value_grad], axis=2).astype(jnp.bfloat16)


def reference(inputs, weight, clip_of_row, out_grad):
    inner_width = HEADS * HEAD
    slot_count = N_PACK * CAP
    projected = jnp.dot(inputs.reshape(FRAMES * ROWS, D), weight, preferred_element_type=jnp.float32)
    features = jnp.concatenate([jax.nn.relu(projected[:, :2 * inner_width]), projected[:, 2 * inner_width:]], axis=1)
    features = features.astype(jnp.bfloat16).reshape(FRAMES, ROWS, 3 * inner_width)
    places = jax.vmap(slot_places)(clip_of_row)
    feat_slots = jax.vmap(place_rows)(features, places).reshape(FRAMES, CLIPS, slot_count, 3, HEADS, HEAD)
    grad_slots = jax.vmap(place_rows)(out_grad, places).reshape(FRAMES, CLIPS, slot_count, HEADS, HEAD)
    block_state, block_norm = lax.map(block_terms, feat_slots)
    state_lo = jnp.cumsum(block_state, axis=0).astype(jnp.bfloat16)
    norm_lo = jnp.cumsum(block_norm, axis=0).astype(jnp.bfloat16)
    attended, numer_grad, denom_grad, grad_block, dnorm_block = lax.map(query_terms, (feat_slots, state_lo, norm_lo, grad_slots))
    grad_lo = jnp.flip(jnp.cumsum(jnp.flip(grad_block, 0), axis=0), 0).astype(jnp.bfloat16)
    dnorm_lo = jnp.flip(jnp.cumsum(jnp.flip(dnorm_block, 0), axis=0), 0).astype(jnp.bfloat16)
    feat_grads = lax.map(back_terms, (feat_slots, numer_grad, denom_grad, state_lo, norm_lo, grad_lo, dnorm_lo))
    attention_out = jax.vmap(take_rows)(attended.reshape(FRAMES, CLIPS * slot_count, inner_width), places)
    grad_rows = jax.vmap(take_rows)(feat_grads.reshape(FRAMES, CLIPS * slot_count, 3 * inner_width), places)
    input_grad = jnp.dot(grad_rows.reshape(FRAMES * ROWS, 3 * inner_width), weight.T, preferred_element_type=jnp.float32)
    return attention_out, input_grad.astype(jnp.bfloat16).reshape(FRAMES, ROWS, D)
```

```python
import jax
import jax.numpy as jnp
from jax import lax
from jax.experimental import pallas as pl
from jax.experimental.pallas import tpu as pltpu
from jax.sharding import PartitionSpec as P

F32 = jnp.float32
BF16 = jnp.bfloat16
MESH = pl.DeviceIdType.MESH
EPS = 1e-06
HEAD = 112
HEADS = 10
WIDE = 128
TOK = 512
D = 2240
HD = HEADS * HEAD
COLS = 3 * HD
FLAT = HEADS * WIDE
RING = 4
QUARTER = FLAT // RING
NROWS = 24


def tn(a, b):
    return lax.dot_general(a, b, (((0,), (0,)), ((), ())), preferred_element_type=F32)


def nt(a, b):
    return lax.dot_general(a, b, (((1,), (1,)), ((), ())), preferred_element_type=F32)


def nn(a, b):
    return lax.dot_general(a, b, (((1,), (0,)), ((), ())), preferred_element_type=F32)


def lanes(shape):
    return lax.broadcasted_iota(jnp.int32, shape, len(shape) - 1)


class Place:
    def __init__(self):
        frame = lax.axis_index("frame")
        pack = lax.axis_index("pack")
        self.x, self.y = frame // RING, frame % RING
        self.z, self.c = pack // 2, pack % 2
        self.frame, self.pack = frame, pack

    def core(self):
        return {"frame": self.frame, "pack": self.z * 2 + (1 - self.c)}

    def along_z(self, j):
        return {"frame": self.frame, "pack": ((self.z + j) % RING) * 2 + self.c}

    def along_y(self, j):
        return {"frame": self.x * RING + (self.y + j) % RING, "pack": self.pack}

    def along_x(self, j):
        return {"frame": ((self.x + j) % RING) * RING + self.y, "pack": self.pack}

    def peers(self):
        out = [self.core()]
        for j in (1, 2, 3):
            out += [self.along_z(j), self.along_y(j), self.along_x(j)]
        return out

    def earlier(self, at, j, reverse):
        return (j > at) if reverse else (j <= at)


class Links:
    def __init__(self, send, recv):
        self.send, self.recv, self.at, self.copies = send, recv, 0, []

    def start(self, src, dst, device):
        copy = pltpu.make_async_remote_copy(
            src_ref=src,
            dst_ref=dst,
            send_sem=self.send.at[self.at],
            recv_sem=self.recv.at[self.at],
            device_id=device,
            device_id_type=MESH,
        )
        self.at += 1
        copy.start()
        self.copies.append(copy)
        return copy

    def drain(self):
        for copy in self.copies:
            copy.wait_send()


class Small:
    def __init__(self, place, links, refs, reverse):
        self.p, self.l, self.reverse = place, links, reverse
        self.own, self.rc, self.sz, self.rz, self.sy, self.ry, self.sx, self.rx, self.inc, self.out = refs

    def s0(self):
        self.w = [self.l.start(self.own, self.rc, self.p.core())]

    def wait(self):
        for w in self.w:
            w.wait_recv()

    def s1(self):
        self.wait()
        self.sz[...] = self.own[...] + self.rc[...]
        self.w = [self.l.start(self.sz, self.rz.at[j - 1], self.p.along_z(j)) for j in (1, 2, 3)]

    def s2(self):
        self.wait()
        self.sy[...] = self.sz[...] + self.rz[0] + self.rz[1] + self.rz[2]
        self.w = [self.l.start(self.sy, self.ry.at[j - 1], self.p.along_y(j)) for j in (1, 2, 3)]

    def s3(self):
        self.wait()
        total = self.sy[...]
        part = total
        for j in (1, 2, 3):
            term = self.ry[j - 1]
            total = total + term
            part = part + jnp.where(self.p.earlier(self.p.y, j, self.reverse), term, 0.0)
        self.sx[...] = total
        self.inc[...] = part
        self.w = [self.l.start(self.sx, self.rx.at[j - 1], self.p.along_x(j)) for j in (1, 2, 3)]

    def s4(self):
        self.wait()
        part = self.inc[...]
        for j in (1, 2, 3):
            part = part + jnp.where(self.p.earlier(self.p.x, j, self.reverse), self.rx[j - 1], 0.0)
        self.out[...] = part.astype(BF16).astype(F32)


class Big:
    def __init__(self, place, links, refs, reverse):
        self.p, self.l, self.reverse = place, links, reverse
        self.acc, self.sc, self.rc, self.sz, self.rz, self.sy, self.ry, self.sx, self.rx, self.inc, self.out = refs

    def put(self, rows, both):
        own, other = both[:, :WIDE], both[:, WIDE:]
        first = self.p.c == 0
        self.acc[rows, :] = jnp.where(first, own, other)
        self.sc[rows, :] = jnp.where(first, other, own).astype(BF16)

    def wait(self):
        for w in self.w:
            w.wait_recv()

    def s0(self):
        self.w = [self.l.start(self.sc, self.rc, self.p.core())]

    def s1(self):
        self.wait()
        for q in range(RING):
            rows = slice(q * QUARTER, (q + 1) * QUARTER)
            total = self.acc[rows, :] + self.rc[rows, :].astype(F32)
            self.acc[rows, :] = total
            self.sz[q] = total.astype(BF16)
        self.w = [
            self.l.start(self.sz.at[(self.p.z + j) % RING], self.rz.at[j - 1], self.p.along_z(j))
            for j in (1, 2, 3)
        ]

    def s2(self):
        self.wait()
        mine = self.acc[pl.ds(pl.multiple_of(self.p.z * QUARTER, 64), QUARTER), :]
        total = mine + self.rz[0].astype(F32) + self.rz[1].astype(F32) + self.rz[2].astype(F32)
        self.inc[...] = total
        self.sy[...] = total.astype(BF16)
        self.w = [self.l.start(self.sy, self.ry.at[j - 1], self.p.along_y(j)) for j in (1, 2, 3)]

    def s3(self):
        self.wait()
        total = self.inc[...]
        part = total
        for j in (1, 2, 3):
            term = self.ry[j - 1].astype(F32)
            total = total + term
            part = part + jnp.where(self.p.earlier(self.p.y, j, self.reverse), term, 0.0)
        self.inc[...] = part
        self.sx[...] = total.astype(BF16)
        self.w = [self.l.start(self.sx, self.rx.at[j - 1], self.p.along_x(j)) for j in (1, 2, 3)]

    def piece(self, clip, quarter):
        return self.out.at[clip, pl.ds(pl.multiple_of(quarter * QUARTER, 64), QUARTER), :]

    def s4(self):
        self.wait()
        part = self.inc[...]
        for j in (1, 2, 3):
            part = part + jnp.where(
                self.p.earlier(self.p.x, j, self.reverse), self.rx[j - 1].astype(F32), 0.0
            )
        here = self.piece(self.p.c, self.p.z)
        here[...] = part.astype(BF16)
        self.w = [self.l.start(here, here, self.p.along_z(j)) for j in (1, 2, 3)]
        self.wc = [self.l.start(here, here, self.p.core())]

    def s5(self):
        for j in (1, 2, 3):
            self.w[j - 1].wait_recv()
            here = self.piece(self.p.c, (self.p.z - j + RING) % RING)
            self.wc.append(self.l.start(here, here, self.p.core()))

    def s6(self):
        for w in self.wc:
            w.wait_recv()


def small_scratch():
    one = pltpu.VMEM((NROWS, WIDE), F32)
    three = pltpu.VMEM((3, NROWS, WIDE), F32)
    return [one, one, one, three, one, three, one, three, one, one]


def big_scratch():
    three = pltpu.VMEM((3, QUARTER, WIDE), BF16)
    one = pltpu.VMEM((QUARTER, WIDE), BF16)
    return [
        pltpu.VMEM((FLAT, WIDE), F32),
        pltpu.VMEM((FLAT, WIDE), BF16),
        pltpu.VMEM((FLAT, WIDE), BF16),
        pltpu.VMEM((RING, QUARTER, WIDE), BF16),
        three,
        one,
        three,
        one,
        three,
        pltpu.VMEM((QUARTER, WIDE), F32),
        pltpu.VMEM((2, FLAT, WIDE), BF16),
    ]


COPIES = 2 * 10 + 2 * 17
SPANS = ((1024, 2304), (2304, COLS), (0, 1024))


def kernel(
    x_hbm, w_hbm, clip_hbm, og_hbm, att_hbm, ig_hbm,
    xv, wv, clipv, ogv, proj, feat, og, ng, inv, m0, m1, dg, grads, acc, outv, attp, attv,
    lsem, send, recv, *rest,
):
    ns, ds_, bs, bg = rest[:10], rest[10:20], rest[20:31], rest[31:42]
    p = Place()
    barrier = pltpu.get_barrier_semaphore()
    peers = p.peers()
    for peer in peers:
        pl.semaphore_signal(barrier, inc=1, device_id=peer, device_id_type=MESH)

    loads = [
        pltpu.make_async_copy(clip_hbm, clipv, lsem.at[0]),
        pltpu.make_async_copy(x_hbm.at[0], xv, lsem.at[1]),
    ]
    for i, (lo, hi) in enumerate(SPANS):
        loads.append(
            pltpu.make_async_copy(w_hbm.at[:, lo:hi], wv.at[:, lo:hi], lsem.at[2 + i])
        )
    loads.append(pltpu.make_async_copy(og_hbm.at[0], ogv, lsem.at[5]))
    for i in (0, 1, 2, 5, 3, 4):
        loads[i].start()

    links = Links(send, recv)
    norm = Small(p, links, ns, False)
    dnorm = Small(p, links, ds_, True)
    state = Big(p, links, bs, False)
    grad = Big(p, links, bg, True)

    def clip_masks():
        loads[0].wait()
        row = clipv[...].astype(F32)
        for t in range(TOK // WIDE):
            tile = jnp.broadcast_to(row[:, t * WIDE : (t + 1) * WIDE], (WIDE, WIDE)).T
            rows = slice(t * WIDE, (t + 1) * WIDE)
            m1[rows, :] = tile.astype(BF16)
            m0[rows, :] = (1.0 - tile).astype(BF16)

    def project(start, count):
        def one(t, carry):
            c0 = pl.multiple_of(start + t * 256, WIDE)
            r = nn(xv[...], wv[:, pl.ds(c0, 256)])
            relu = c0 + lanes(r.shape) < 2 * HD
            proj[:, pl.ds(c0, 256)] = jnp.where(relu, jnp.maximum(r, 0.0), r).astype(BF16)
            return carry

        lax.fori_loop(0, count, one, 0)

    def project_tail():
        proj[:, 3328:COLS] = nn(xv[...], wv[:, 3328:COLS]).astype(BF16)

    def expand(src, width, head, dst, at):
        tile, off = (HEAD * head) // WIDE, (HEAD * head) % WIDE
        lo = src[:, tile * WIDE : min((tile + 1) * WIDE, width)]
        lane = lanes((TOK, WIDE))
        if off > WIDE - HEAD:
            hi = src[:, (tile + 1) * WIDE : min((tile + 2) * WIDE, width)].astype(F32)
            if hi.shape[1] < WIDE:
                hi = jnp.concatenate([hi, jnp.zeros((TOK, WIDE - hi.shape[1]), F32)], axis=1)
            lo = jnp.where(lane >= off, lo.astype(F32), hi)
        else:
            lo = lo.astype(F32)
        if off:
            lo = pltpu.roll(lo, WIDE - off, 1)
        dst[at] = jnp.where(lane < HEAD, lo, 0.0).astype(BF16)

    def expand_feat(lo, hi):
        for head in range(lo, hi):
            expand(proj, 3456, head, feat, head)

    def masked(v):
        return jnp.concatenate([v * m0[...], v * m1[...]], axis=1)

    def rows_of(h):
        return pl.ds(pl.multiple_of(h * WIDE, WIDE), WIDE)

    def clip_sums(ref, h, v):
        ref[pl.ds(h, 1), :] = jnp.sum(v * m0[...].astype(F32), axis=0, keepdims=True)
        ref[pl.ds(HEADS + h, 1), :] = jnp.sum(v * m1[...].astype(F32), axis=0, keepdims=True)

    def norm_local():
        norm.own[...] = jnp.zeros_like(norm.own)

        def one(h, carry):
            clip_sums(norm.own, h, feat[HEADS + h].astype(F32))
            return carry

        lax.fori_loop(0, HEADS, one, 0)

    def state_local():
        def one(h, carry):
            state.put(rows_of(h), tn(feat[HEADS + h], masked(feat[2 * HEADS + h])))
            return carry

        lax.fori_loop(0, HEADS, one, 0)

    def grad_local():
        def one(h, carry):
            q = feat[h]
            n0 = norm.out[pl.ds(h, 1), :].astype(BF16)
            n1 = norm.out[pl.ds(HEADS + h, 1), :].astype(BF16)
            side = jnp.concatenate(
                [jnp.broadcast_to(n0, (WIDE, WIDE)), jnp.broadcast_to(n1, (WIDE, WIDE))], axis=1
            )
            r = 1.0 / (nt(masked(q), side) + EPS)
            inv[h] = r
            g = (og[h].astype(F32) * r).astype(BF16)
            ng[h] = g
            grad.put(rows_of(h), tn(q, masked(g)))
            return carry

        lax.fori_loop(0, HEADS, one, 0)

    def attend():
        dnorm.own[...] = jnp.zeros_like(dnorm.own)

        def one(h, carry):
            q = feat[h]
            s0, s1 = state.out[0, rows_of(h), :], state.out[1, rows_of(h), :]
            r = inv[h]
            att = nn(masked(q), jnp.concatenate([s0, s1], axis=0)) * r
            attp[h] = att.astype(BF16)
            d = -jnp.sum(og[h].astype(F32) * att, axis=1, keepdims=True) * r
            q32 = q.astype(F32)
            clip_sums(dnorm.own, h, q32 * d)
            n0, n1 = norm.out[pl.ds(h, 1), :], norm.out[pl.ds(HEADS + h, 1), :]
            qg = nt(masked(ng[h]), jnp.concatenate([s0, s1], axis=1))
            qg = qg + d * jnp.where(m1[...].astype(F32) > 0, n1, n0)
            dg[h] = jnp.where(q32 > 0, qg, 0.0).astype(BF16)
            return carry

        lax.fori_loop(0, HEADS, one, 0)

    def value_grads():
        def one(h, carry):
            g0, g1 = grad.out[0, rows_of(h), :], grad.out[1, rows_of(h), :]
            k = feat[HEADS + h]
            dg[2 * HEADS + h] = nn(masked(k), jnp.concatenate([g0, g1], axis=0)).astype(BF16)
            return carry

        lax.fori_loop(0, HEADS, one, 0)

    def key_grads():
        def one(h, carry):
            g0, g1 = grad.out[0, rows_of(h), :], grad.out[1, rows_of(h), :]
            kg = nt(masked(feat[2 * HEADS + h]), jnp.concatenate([g0, g1], axis=1))
            d0, d1 = dnorm.out[pl.ds(h, 1), :], dnorm.out[pl.ds(HEADS + h, 1), :]
            kg = kg + jnp.where(m1[...].astype(F32) > 0, d1, d0)
            keep = feat[HEADS + h].astype(F32) > 0
            dg[HEADS + h] = jnp.where(keep, kg, 0.0).astype(BF16)
            return carry

        lax.fori_loop(0, HEADS, one, 0)

    def flat_tile(src, tile):
        head, off = (WIDE * tile) // HEAD, (WIDE * tile) % HEAD
        count = HEAD - off
        a = src[head].astype(F32)
        if off:
            a = pltpu.roll(a, WIDE - off, 1)
        if head + 1 < src.shape[0]:
            b = pltpu.roll(src[head + 1].astype(F32), count, 1)
            a = jnp.where(lanes(a.shape) < count, a, b)
        return a.astype(BF16)

    def flatten_grads(lo, hi):
        for tile in range(lo, hi):
            width = min(WIDE, COLS - tile * WIDE)
            grads[:, tile * WIDE : tile * WIDE + width] = flat_tile(dg, tile)[:, :width]

    def back(lo, hi, kind):
        def step(n0, count):
            r = nt(grads[:, lo:hi], wv[pl.ds(n0, count), lo:hi])
            at = (slice(None), pl.ds(n0, count))
            if kind > 0:
                r = r + acc[at]
            if kind < 2:
                acc[at] = r
            else:
                outv[at] = r.astype(BF16)

        def one(t, carry):
            step(pl.multiple_of(t * 256, 256), 256)
            return carry

        lax.fori_loop(0, D // 256, one, 0)
        step((D // 256) * 256, D % 256)

    clip_masks()
    loads[1].wait()
    loads[2].wait()
    project(1024, 5)
    expand_feat(HEADS, 2 * HEADS)
    norm_local()
    pl.semaphore_wait(barrier, len(peers))
    norm.s0()
    loads[3].wait()
    project(2304, 1)
    norm.s1()
    project(2560, 3)
    project_tail()
    norm.s2()
    expand_feat(2 * HEADS, 3 * HEADS)
    state_local()
    state.s0()
    norm.s3()
    loads[4].wait()
    project(0, 1)
    state.s1()
    project(256, 3)
    norm.s4()
    state.s2()
    expand_feat(0, HEADS)
    loads[5].wait()
    for head in range(HEADS):
        expand(ogv, HD, head, og, head)
    grad_local()
    grad.s0()
    state.s3()
    grad.s1()
    state.s4()
    grad.s2()
    state.s5()
    grad.s3()
    state.s6()
    attend()
    dnorm.s0()
    grad.s4()
    flatten_grads(0, 8)
    for tile in range(9):
        width = min(WIDE, HD - tile * WIDE)
        attv[:, tile * WIDE : tile * WIDE + width] = flat_tile(attp, tile)[:, :width]
    stores = [pltpu.make_async_copy(attv, att_hbm.at[0], lsem.at[0])]
    stores[0].start()
    dnorm.s1()
    grad.s5()
    back(0, 1024, 0)
    dnorm.s2()
    grad.s6()
    value_grads()
    dnorm.s3()
    flatten_grads(18, 27)
    back(2304, COLS, 1)
    dnorm.s4()
    key_grads()
    flatten_grads(8, 18)
    back(1024, 2304, 2)
    stores.append(pltpu.make_async_copy(outv, ig_hbm.at[0], lsem.at[1]))
    stores[1].start()
    links.drain()
    for store in stores:
        store.wait()


def per_device(inputs, weight, clip_of_row, out_grad):
    anywhere = pl.BlockSpec(memory_space=pl.ANY)
    heads = lambda n, t: pltpu.VMEM((n, TOK, WIDE), t)
    return pl.pallas_call(
        kernel,
        out_shape=(
            jax.ShapeDtypeStruct((1, TOK, HD), BF16),
            jax.ShapeDtypeStruct((1, TOK, D), BF16),
        ),
        in_specs=[anywhere] * 4,
        out_specs=(anywhere, anywhere),
        scratch_shapes=[
            pltpu.VMEM((TOK, D), BF16),
            pltpu.VMEM((D, COLS), BF16),
            pltpu.VMEM((1, TOK), jnp.int32),
            pltpu.VMEM((TOK, HD), BF16),
            pltpu.VMEM((TOK, 3456), BF16),
            heads(3 * HEADS, BF16),
            heads(HEADS, BF16),
            heads(HEADS, BF16),
            heads(HEADS, F32),
            pltpu.VMEM((TOK, WIDE), BF16),
            pltpu.VMEM((TOK, WIDE), BF16),
            heads(3 * HEADS, BF16),
            pltpu.VMEM((TOK, COLS), BF16),
            pltpu.VMEM((TOK, D), F32),
            pltpu.VMEM((TOK, D), BF16),
            heads(HEADS, BF16),
            pltpu.VMEM((TOK, HD), BF16),
            pltpu.SemaphoreType.DMA((6,)),
            pltpu.SemaphoreType.DMA((COPIES,)),
            pltpu.SemaphoreType.DMA((COPIES,)),
            *small_scratch(),
            *small_scratch(),
            *big_scratch(),
            *big_scratch(),
        ],
        compiler_params=pltpu.CompilerParams(
            collective_id=0, has_side_effects=True, vmem_limit_bytes=67000000
        ),
    )(inputs, weight, clip_of_row, out_grad)


def solution(mesh):
    placed = (P("frame", "pack", None), P(), P("frame", "pack"), P("frame", "pack", None))
    return jax.shard_map(
        per_device,
        mesh=mesh,
        in_specs=placed,
        out_specs=(P("frame", "pack", None), P("frame", "pack", None)),
        check_vma=False,
    )
```

```python
import jax
import jax.numpy as jnp
from jax import lax
from jax.experimental import pallas as pl
from jax.experimental.pallas import tpu as pltpu
from jax.sharding import PartitionSpec as P

F32 = jnp.float32
BF16 = jnp.bfloat16
MESH = pl.DeviceIdType.MESH
EPS = 1e-06
HEAD = 112
HEADS = 10
WIDE = 128
TOK = 512
D = 2240
HD = HEADS * HEAD
COLS = 3 * HD
RING = 4
GROUPS = 2
PER = HEADS // GROUPS
ROWS = 576
QUARTER = ROWS // RING
NROWS = 24
TILES = 9


def tn(a, b):
    return lax.dot_general(a, b, (((0,), (0,)), ((), ())), preferred_element_type=F32)


def nt(a, b):
    return lax.dot_general(a, b, (((1,), (1,)), ((), ())), preferred_element_type=F32)


def nn(a, b):
    return lax.dot_general(a, b, (((1,), (0,)), ((), ())), preferred_element_type=F32)


class Place:
    def __init__(self):
        frame = lax.axis_index("frame")
        pack = lax.axis_index("pack")
        self.x, self.y = frame // RING, frame % RING
        self.z, self.c = pack // 2, pack % 2
        self.frame, self.pack = frame, pack

    def core(self):
        return {"frame": self.frame, "pack": self.z * 2 + (1 - self.c)}

    def along_z(self, j):
        return {"frame": self.frame, "pack": ((self.z + j) % RING) * 2 + self.c}

    def along_y(self, j):
        return {"frame": self.x * RING + (self.y + j) % RING, "pack": self.pack}

    def along_x(self, j):
        return {"frame": ((self.x + j) % RING) * RING + self.y, "pack": self.pack}

    def peers(self):
        out = [self.core()]
        for j in (1, 2, 3):
            out += [self.along_z(j), self.along_y(j), self.along_x(j)]
        return out

    def earlier(self, at, j, reverse):
        return (j > at) if reverse else (j <= at)


class Links:
    def __init__(self, send, recv):
        self.send, self.recv, self.at, self.copies = send, recv, 0, []

    def start(self, src, dst, device):
        copy = pltpu.make_async_remote_copy(
            src_ref=src,
            dst_ref=dst,
            send_sem=self.send.at[self.at],
            recv_sem=self.recv.at[self.at],
            device_id=device,
            device_id_type=MESH,
        )
        self.at += 1
        copy.start()
        self.copies.append(copy)
        return copy

    def drain(self):
        for copy in self.copies:
            copy.wait_send()


class Small:
    def __init__(self, place, links, refs, reverse):
        self.p, self.l, self.reverse = place, links, reverse
        self.own, self.rc, self.sz, self.rz, self.sy, self.ry, self.sx, self.rx, self.inc, self.out = refs

    def s0(self):
        self.w = [self.l.start(self.own, self.rc, self.p.core())]

    def wait(self):
        for w in self.w:
            w.wait_recv()

    def s1(self):
        self.wait()
        self.sz[...] = self.own[...] + self.rc[...]
        self.w = [self.l.start(self.sz, self.rz.at[j - 1], self.p.along_z(j)) for j in (1, 2, 3)]

    def s2(self):
        self.wait()
        self.sy[...] = self.sz[...] + self.rz[0] + self.rz[1] + self.rz[2]
        self.w = [self.l.start(self.sy, self.ry.at[j - 1], self.p.along_y(j)) for j in (1, 2, 3)]

    def s3(self):
        self.wait()
        total = self.sy[...]
        part = total
        for j in (1, 2, 3):
            term = self.ry[j - 1]
            total = total + term
            part = part + jnp.where(self.p.earlier(self.p.y, j, self.reverse), term, 0.0)
        self.sx[...] = total
        self.inc[...] = part
        self.w = [self.l.start(self.sx, self.rx.at[j - 1], self.p.along_x(j)) for j in (1, 2, 3)]

    def s4(self):
        self.wait()
        part = self.inc[...]
        for j in (1, 2, 3):
            part = part + jnp.where(self.p.earlier(self.p.x, j, self.reverse), self.rx[j - 1], 0.0)
        self.out[...] = part.astype(BF16).astype(F32)


class Big:
    def __init__(self, place, links, refs, reverse):
        self.p, self.l, self.reverse = place, links, reverse
        self.acc, self.sc, self.rc, self.sz, self.rz, self.sy, self.ry, self.sx, self.rx, self.inc, self.out = refs

    def put(self, i, both):
        both = jnp.concatenate([both, jnp.zeros((2 * HEAD, WIDE - HEAD), F32)], axis=1)
        own, other = both[:HEAD], both[HEAD:]
        first = self.p.c == 0
        rows = slice(i * HEAD, (i + 1) * HEAD)
        self.acc[rows, :] = jnp.where(first, own, other)
        self.sc[rows, :] = jnp.where(first, other, own).astype(BF16)

    def clear(self):
        rows = slice(PER * HEAD, ROWS)
        self.acc[rows, :] = jnp.zeros((ROWS - PER * HEAD, WIDE), F32)
        self.sc[rows, :] = jnp.zeros((ROWS - PER * HEAD, WIDE), BF16)

    def pair(self, i):
        rows = slice(i * HEAD, (i + 1) * HEAD)
        return self.out[0, rows, :], self.out[1, rows, :]

    def wait(self):
        for w in self.w:
            w.wait_recv()

    def s0(self):
        self.w = [self.l.start(self.sc, self.rc, self.p.core())]

    def s1(self):
        self.wait()
        for q in range(RING):
            rows = slice(q * QUARTER, (q + 1) * QUARTER)
            total = self.acc[rows, :] + self.rc[rows, :].astype(F32)
            self.acc[rows, :] = total
            self.sz[q] = total.astype(BF16)
        self.w = [
            self.l.start(self.sz.at[(self.p.z + j) % RING], self.rz.at[j - 1], self.p.along_z(j))
            for j in (1, 2, 3)
        ]

    def s2(self):
        self.wait()
        mine = self.acc[pl.ds(pl.multiple_of(self.p.z * QUARTER, 16), QUARTER), :]
        total = mine + self.rz[0].astype(F32) + self.rz[1].astype(F32) + self.rz[2].astype(F32)
        self.inc[...] = total
        self.sy[...] = total.astype(BF16)
        self.w = [self.l.start(self.sy, self.ry.at[j - 1], self.p.along_y(j)) for j in (1, 2, 3)]

    def s3(self):
        self.wait()
        total = self.inc[...]
        part = total
        for j in (1, 2, 3):
            term = self.ry[j - 1].astype(F32)
            total = total + term
            part = part + jnp.where(self.p.earlier(self.p.y, j, self.reverse), term, 0.0)
        self.inc[...] = part
        self.sx[...] = total.astype(BF16)
        self.w = [self.l.start(self.sx, self.rx.at[j - 1], self.p.along_x(j)) for j in (1, 2, 3)]

    def piece(self, clip, quarter):
        return self.out.at[clip, pl.ds(pl.multiple_of(quarter * QUARTER, 16), QUARTER), :]

    def s4(self):
        self.wait()
        part = self.inc[...]
        for j in (1, 2, 3):
            part = part + jnp.where(
                self.p.earlier(self.p.x, j, self.reverse), self.rx[j - 1].astype(F32), 0.0
            )
        here = self.piece(self.p.c, self.p.z)
        here[...] = part.astype(BF16)
        self.w = [self.l.start(here, here, self.p.along_z(j)) for j in (1, 2, 3)]
        self.wc = [self.l.start(here, here, self.p.core())]

    def s5(self):
        for j in (1, 2, 3):
            self.w[j - 1].wait_recv()
            here = self.piece(self.p.c, (self.p.z - j + RING) % RING)
            self.wc.append(self.l.start(here, here, self.p.core()))

    def s6(self):
        for w in self.wc:
            w.wait_recv()


def small_scratch():
    one = pltpu.VMEM((NROWS, WIDE), F32)
    three = pltpu.VMEM((3, NROWS, WIDE), F32)
    return [one, one, one, three, one, three, one, three, one, one]


def big_scratch():
    three = pltpu.VMEM((3, QUARTER, WIDE), BF16)
    one = pltpu.VMEM((QUARTER, WIDE), BF16)
    return [
        pltpu.VMEM((ROWS, WIDE), F32),
        pltpu.VMEM((ROWS, WIDE), BF16),
        pltpu.VMEM((ROWS, WIDE), BF16),
        pltpu.VMEM((RING, QUARTER, WIDE), BF16),
        three,
        one,
        three,
        one,
        three,
        pltpu.VMEM((QUARTER, WIDE), F32),
        pltpu.VMEM((2, ROWS, WIDE), BF16),
    ]


COPIES = 2 * 10 + 2 * GROUPS * 17
SPANS = ((1024, 1664), (1664, 2304), (2304, 2816), (2816, COLS), (0, 640), (640, 1024))


def row_of(h):
    return slice(h * HEAD, (h + 1) * HEAD)


def in_head(rows):
    shape = (rows, HD)
    lane = lax.broadcasted_iota(jnp.int32, shape, 1)
    low = lax.broadcasted_iota(jnp.int32, shape, 0) * HEAD
    return jnp.logical_and(lane >= low, lane < low + HEAD)


def kernel(
    x_hbm, w_hbm, clip_hbm, og_hbm, att_hbm, ig_hbm,
    xv, wv, clipv, og, feat, ng, inv, dgs, grads, acc, outv, attv, ncol, dcol,
    lsem, send, recv, *rest,
):
    ns, ds_ = rest[:10], rest[10:20]
    bigs = [rest[20 + 11 * i : 31 + 11 * i] for i in range(2 * GROUPS)]
    p = Place()
    barrier = pltpu.get_barrier_semaphore()
    peers = p.peers()
    for peer in peers:
        pl.semaphore_signal(barrier, inc=1, device_id=peer, device_id_type=MESH)

    loads = {
        "clip": pltpu.make_async_copy(clip_hbm, clipv, lsem.at[0]),
        "x": pltpu.make_async_copy(x_hbm.at[0], xv, lsem.at[1]),
        "og": pltpu.make_async_copy(og_hbm.at[0], og, lsem.at[2]),
    }
    for i, (lo, hi) in enumerate(SPANS):
        loads[lo] = pltpu.make_async_copy(w_hbm.at[:, lo:hi], wv.at[:, lo:hi], lsem.at[3 + i])
    for name in ("clip", "x", 1024, 1664, 2304, 2816, 0, 640, "og"):
        loads[name].start()

    links = Links(send, recv)
    norm = Small(p, links, ns, False)
    dnorm = Small(p, links, ds_, True)
    state = [Big(p, links, bigs[g], False) for g in range(GROUPS)]
    grad = [Big(p, links, bigs[GROUPS + g], True) for g in range(GROUPS)]

    def project(lo, hi):
        r = tn(wv[:, lo:hi], xv[...])
        pos = min(max(2 * HD - lo, 0), hi - lo)
        if pos:
            feat[lo : lo + pos, :] = jnp.maximum(r[:pos], 0.0).astype(BF16)
        if pos < hi - lo:
            feat[lo + pos : hi, :] = r[pos:].astype(BF16)

    for b in state + grad:
        b.clear()
    loads["clip"].wait()
    is1 = clipv[...] > 0
    m1 = clipv[...].astype(F32)
    m0 = 1.0 - m1
    m0b, m1b = m0.astype(BF16), m1.astype(BF16)

    def split(v, gap=0):
        parts = [v * m0b, v * m1b]
        if gap:
            zero = jnp.zeros((gap, TOK), BF16)
            parts = [parts[0], zero, parts[1], zero]
        return jnp.concatenate(parts, axis=0)

    def put_rows(ref, r):
        ref[...] = jnp.zeros_like(ref)
        for t in range(TILES):
            width = min(WIDE, HD - t * WIDE)
            ref[2 * t : 2 * t + 2, :width] = r[0:2, t * WIDE : t * WIDE + width]

    def get_rows(ref):
        return jnp.concatenate([ref[2 * t : 2 * t + 2, :] for t in range(TILES)], axis=1)

    def columns(ref, dst):
        for t in range(TILES):
            both = ref[2 * t : 2 * t + 2, :]
            both = jnp.concatenate([both, jnp.zeros((6, WIDE), F32)], axis=0)
            dst[t * WIDE : (t + 1) * WIDE, :] = both.T

    def pick(col, h):
        c = col[row_of(h), :]
        return jnp.where(is1, c[:, 1:2], c[:, 0:1])

    def norm_local():
        side = jnp.concatenate([m0b, m1b, jnp.zeros((14, TOK), BF16)], axis=0)
        put_rows(norm.own, nt(side, feat[HD : 2 * HD, :]))

    def state_local(g):
        for i in range(PER):
            h = g * PER + i
            k, v = feat[row_of(HEADS + h), :], feat[row_of(2 * HEADS + h), :]
            state[g].put(i, nt(split(k), v))

    def denominators():
        rows = get_rows(norm.out)[:, :HD]
        keep = in_head(16)
        side = jnp.concatenate(
            [jnp.where(keep, jnp.broadcast_to(rows[c : c + 1], (16, HD)), 0.0) for c in (0, 1)], axis=0
        )
        den = nn(side.astype(BF16), feat[:HD, :])
        inv[...] = 1.0 / (jnp.where(is1, den[16:], den[:16]) + EPS)
        columns(norm.out, ncol)

    def grad_local(g):
        for i in range(PER):
            h = g * PER + i
            v = (og[row_of(h), :].astype(F32) * inv[h : h + 1, :]).astype(BF16)
            ng[row_of(h), :] = v
            grad[g].put(i, nt(split(feat[row_of(h), :]), v))

    def attend(g):
        for i in range(PER):
            h = g * PER + i
            q = feat[row_of(h), :]
            s0, s1 = state[g].pair(i)
            r = inv[h : h + 1, :]
            att = tn(jnp.concatenate([s0, s1], axis=0), split(q))[:HEAD] * r
            attv[row_of(h), :] = att.astype(BF16)
            d = -jnp.sum(og[row_of(h), :].astype(F32) * att, axis=0, keepdims=True) * r
            dgs[h : h + 1, :] = d
            qg = nn(jnp.concatenate([s0, s1], axis=1), split(ng[row_of(h), :], WIDE - HEAD))
            qg = qg + d * pick(ncol, h)
            grads[row_of(h), :] = jnp.where(q.astype(F32) > 0, qg, 0.0).astype(BF16)

    def dnorm_local():
        d = dgs[...]
        both = jnp.concatenate([d * m0, d * m1], axis=0)
        hi = both.astype(BF16)
        lo = (both - hi.astype(F32)).astype(BF16)
        r = nt(jnp.concatenate([hi, lo], axis=0), feat[:HD, :])
        r = r[:32] + r[32:]
        keep = in_head(16)
        rows = [
            jnp.sum(jnp.where(keep, r[16 * c : 16 * c + 16], 0.0), axis=0, keepdims=True) for c in (0, 1)
        ]
        put_rows(dnorm.own, jnp.concatenate(rows, axis=0))

    def value_grads(g):
        for i in range(PER):
            h = g * PER + i
            g0, g1 = grad[g].pair(i)
            r = tn(jnp.concatenate([g0, g1], axis=0), split(feat[row_of(HEADS + h), :]))
            grads[row_of(2 * HEADS + h), :] = r[:HEAD].astype(BF16)

    def key_grads(g):
        for i in range(PER):
            h = g * PER + i
            g0, g1 = grad[g].pair(i)
            v = feat[row_of(2 * HEADS + h), :]
            kg = nn(jnp.concatenate([g0, g1], axis=1), split(v, WIDE - HEAD)) + pick(dcol, h)
            keep = feat[row_of(HEADS + h), :].astype(F32) > 0
            grads[row_of(HEADS + h), :] = jnp.where(keep, kg, 0.0).astype(BF16)

    def back(lo, hi, kind, then=None):
        for m in (0, 1):
            rows = slice(m * HD, (m + 1) * HD)
            r = nn(wv[rows, lo:hi], grads[lo:hi, :])
            if kind > 0:
                r = r + acc[rows, :]
            if kind < 2:
                acc[rows, :] = r
            else:
                outv[rows, :] = r.astype(BF16)
                then(m, rows)

    stores = []

    def store(src, dst, at):
        stores.append(pltpu.make_async_copy(src, dst, lsem.at[at]))
        stores[-1].start()

    loads["x"].wait()
    for lo, hi in SPANS[:2]:
        loads[lo].wait()
        project(lo, hi)
    norm_local()
    pl.semaphore_wait(barrier, len(peers))
    norm.s0()
    loads[2304].wait()
    project(2304, 2816)
    norm.s1()
    state_local(0)
    state[0].s0()
    loads[2816].wait()
    project(2816, COLS)
    norm.s2()
    state[0].s1()
    state_local(1)
    state[1].s0()
    loads[0].wait()
    project(0, 640)
    norm.s3()
    state[1].s1()
    state[0].s2()
    loads[640].wait()
    project(640, 1024)
    state[1].s2()
    norm.s4()
    loads["og"].wait()
    denominators()
    state[0].s3()
    grad_local(0)
    grad[0].s0()
    state[1].s3()
    grad_local(1)
    grad[1].s0()
    grad[0].s1()
    state[0].s4()
    grad[1].s1()
    state[1].s4()
    grad[0].s2()
    state[0].s5()
    grad[1].s2()
    state[1].s5()
    grad[0].s3()
    state[0].s6()
    attend(0)
    grad[1].s3()
    state[1].s6()
    attend(1)
    store(attv, att_hbm.at[0], 0)
    dnorm_local()
    dnorm.s0()
    grad[0].s4()
    grad[1].s4()
    dnorm.s1()
    grad[0].s5()
    grad[1].s5()
    back(0, 1024, 0)
    dnorm.s2()
    grad[0].s6()
    value_grads(0)
    grad[1].s6()
    dnorm.s3()
    value_grads(1)
    back(2304, COLS, 1)
    dnorm.s4()
    columns(dnorm.out, dcol)
    key_grads(0)
    key_grads(1)
    back(1024, 2304, 2, lambda m, rows: store(outv.at[rows, :], ig_hbm.at[0, rows, :], 1 + m))
    links.drain()
    for s in stores:
        s.wait()


def per_device(inputs, weight, clip_of_row, out_grad):
    anywhere = pl.BlockSpec(memory_space=pl.ANY)
    bigs = [r for _ in range(2 * GROUPS) for r in big_scratch()]
    att, grad = pl.pallas_call(
        kernel,
        out_shape=(
            jax.ShapeDtypeStruct((1, HD, TOK), BF16),
            jax.ShapeDtypeStruct((1, D, TOK), BF16),
        ),
        in_specs=[anywhere] * 4,
        out_specs=(anywhere, anywhere),
        scratch_shapes=[
            pltpu.VMEM((D, TOK), BF16),
            pltpu.VMEM((D, COLS), BF16),
            pltpu.VMEM((1, TOK), jnp.int32),
            pltpu.VMEM((HD, TOK), BF16),
            pltpu.VMEM((COLS, TOK), BF16),
            pltpu.VMEM((HD, TOK), BF16),
            pltpu.VMEM((16, TOK), F32),
            pltpu.VMEM((16, TOK), F32),
            pltpu.VMEM((COLS, TOK), BF16),
            pltpu.VMEM((D, TOK), F32),
            pltpu.VMEM((D, TOK), BF16),
            pltpu.VMEM((HD, TOK), BF16),
            pltpu.VMEM((TILES * WIDE, 8), F32),
            pltpu.VMEM((TILES * WIDE, 8), F32),
            pltpu.SemaphoreType.DMA((9,)),
            pltpu.SemaphoreType.DMA((COPIES,)),
            pltpu.SemaphoreType.DMA((COPIES,)),
            *small_scratch(),
            *small_scratch(),
            *bigs,
        ],
        compiler_params=pltpu.CompilerParams(
            collective_id=0, has_side_effects=True, vmem_limit_bytes=67000000
        ),
    )(inputs.swapaxes(1, 2), weight, clip_of_row, out_grad.swapaxes(1, 2))
    return att.swapaxes(1, 2), grad.swapaxes(1, 2)


def solution(mesh):
    placed = (P("frame", "pack", None), P(), P("frame", "pack"), P("frame", "pack", None))
    return jax.shard_map(
        per_device,
        mesh=mesh,
        in_specs=placed,
        out_specs=(P("frame", "pack", None), P("frame", "pack", None)),
        check_vma=False,
    )
```

```python
import jax
import jax.numpy as jnp
from jax import lax
from jax.experimental import pallas as pl
from jax.experimental.pallas import tpu as pltpu
from jax.sharding import PartitionSpec as P

F32 = jnp.float32
BF16 = jnp.bfloat16
MESH = pl.DeviceIdType.MESH
EPS = 1e-06
HEAD = 112
HEADS = 10
WIDE = 128
TOK = 512
D = 2240
HD = HEADS * HEAD
COLS = 3 * HD
RING = 4
PACK = 2 * RING
FRAMES = RING * RING
GROUPS = 2
PER = HEADS // GROUPS
ROWS = 576
QUARTER = ROWS // RING
NROWS = 24
TILES = 9


def tn(a, b):
    return lax.dot_general(a, b, (((0,), (0,)), ((), ())), preferred_element_type=F32)


def nt(a, b):
    return lax.dot_general(a, b, (((1,), (1,)), ((), ())), preferred_element_type=F32)


def nn(a, b):
    return lax.dot_general(a, b, (((1,), (0,)), ((), ())), preferred_element_type=F32)


class Place:
    def __init__(self):
        self.frame = lax.axis_index("frame")
        self.pack = lax.axis_index("pack")
        self.z, self.c = self.pack // 2, self.pack % 2

    def pack_peer(self, k):
        dz, flip = divmod(k + 1, 2)
        z = (self.z + dz) % RING
        c = (self.c + flip) % 2
        return {"frame": self.frame, "pack": z * 2 + c}, z, c

    def frame_peer(self, j):
        return {"frame": (self.frame + j + FRAMES) % FRAMES, "pack": self.pack}

    def peers(self):
        return [self.pack_peer(k)[0] for k in range(PACK - 1)] + [
            self.frame_peer(j) for j in range(1, FRAMES)
        ]


class Links:
    def __init__(self, send, recv):
        self.send, self.recv, self.at, self.copies = send, recv, 0, []

    def start(self, src, dst, device, when=None):
        copy = pltpu.make_async_remote_copy(
            src_ref=src,
            dst_ref=dst,
            send_sem=self.send.at[self.at],
            recv_sem=self.recv.at[self.at],
            device_id=device,
            device_id_type=MESH,
        )
        self.at += 1
        if when is None:
            copy.start()
        else:
            pl.when(when)(copy.start)
        self.copies.append((copy, when))
        return copy

    def drain(self):
        for copy, when in self.copies:
            if when is None:
                copy.wait_send()
            else:
                pl.when(when)(copy.wait_send)


class Frames:
    def __init__(self, place, links, reverse):
        self.p, self.l, self.reverse = place, links, reverse

    def spread(self, src, slots):
        f = self.p.frame
        self.w = []
        for j in range(1, FRAMES):
            to, into = (f >= j, f + j < FRAMES) if self.reverse else (f + j < FRAMES, f >= j)
            peer = self.p.frame_peer(-j if self.reverse else j)
            self.w.append((self.l.start(src, slots.at[j - 1], peer, to), into))

    def total(self, own, slots):
        for copy, into in self.w:
            pl.when(into)(copy.wait_recv)
        for j, (_, into) in enumerate(self.w):
            own = own + jnp.where(into, slots[j].astype(F32), 0.0)
        return own


class Small(Frames):
    def __init__(self, place, links, refs, reverse):
        super().__init__(place, links, reverse)
        self.own, self.rz, self.sy, self.ry, self.out = refs

    def s0(self):
        self.wp = [
            self.l.start(self.own, self.rz.at[k], self.p.pack_peer(k)[0]) for k in range(PACK - 1)
        ]

    def s1(self):
        for w in self.wp:
            w.wait_recv()
        total = self.own[...]
        for k in range(PACK - 1):
            total = total + self.rz[k]
        self.sy[...] = total
        self.spread(self.sy, self.ry)

    def s2(self):
        self.out[...] = self.total(self.sy[...], self.ry).astype(BF16).astype(F32)


class Big(Frames):
    def __init__(self, place, links, refs, reverse):
        super().__init__(place, links, reverse)
        self.acc, self.sz, self.rz, self.inc, self.sy, self.ry, self.out = refs

    def put(self, i, both):
        both = jnp.concatenate([both, jnp.zeros((2 * HEAD, WIDE - HEAD), F32)], axis=1)
        rows = slice(i * HEAD, (i + 1) * HEAD)
        self.acc[rows, :] = jnp.where(self.p.c == 0, both[:HEAD], both[HEAD:])
        self.sz[0, rows, :] = both[:HEAD].astype(BF16)
        self.sz[1, rows, :] = both[HEAD:].astype(BF16)

    def clear(self):
        rows = slice(PER * HEAD, ROWS)
        self.acc[rows, :] = jnp.zeros((ROWS - PER * HEAD, WIDE), F32)
        for c in (0, 1):
            self.sz[c, rows, :] = jnp.zeros((ROWS - PER * HEAD, WIDE), BF16)

    def pair(self, i):
        rows = slice(i * HEAD, (i + 1) * HEAD)
        return self.out[0, rows, :], self.out[1, rows, :]

    def quarter(self, z):
        return pl.ds(pl.multiple_of(z * QUARTER, 16), QUARTER)

    def s0(self):
        self.wp = []
        for k in range(PACK - 1):
            peer, z, c = self.p.pack_peer(k)
            self.wp.append(self.l.start(self.sz.at[c, self.quarter(z), :], self.rz.at[k], peer))

    def s1(self):
        for w in self.wp:
            w.wait_recv()
        total = self.acc[self.quarter(self.p.z), :]
        for k in range(PACK - 1):
            total = total + self.rz[k].astype(F32)
        self.inc[...] = total
        self.sy[...] = total.astype(BF16)
        self.spread(self.sy, self.ry)

    def s2(self):
        here = self.out.at[self.p.c, self.quarter(self.p.z), :]
        here[...] = self.total(self.inc[...], self.ry).astype(BF16)
        self.wp = [self.l.start(here, here, self.p.pack_peer(k)[0]) for k in range(PACK - 1)]

    def s3(self):
        for w in self.wp:
            w.wait_recv()


def small_scratch():
    one = pltpu.VMEM((NROWS, WIDE), F32)
    return [one, pltpu.VMEM((PACK - 1, NROWS, WIDE), F32), one, pltpu.VMEM((FRAMES - 1, NROWS, WIDE), F32), one]


def big_scratch():
    return [
        pltpu.VMEM((ROWS, WIDE), F32),
        pltpu.VMEM((2, ROWS, WIDE), BF16),
        pltpu.VMEM((PACK - 1, QUARTER, WIDE), BF16),
        pltpu.VMEM((QUARTER, WIDE), F32),
        pltpu.VMEM((QUARTER, WIDE), BF16),
        pltpu.VMEM((FRAMES - 1, QUARTER, WIDE), BF16),
        pltpu.VMEM((2, ROWS, WIDE), BF16),
    ]


COPIES = 2 * (PACK - 1 + FRAMES - 1) + 2 * GROUPS * (2 * (PACK - 1) + FRAMES - 1)
SPANS = ((1024, 1664), (1664, 2304), (2304, 2816), (2816, COLS), (0, 640), (640, 1024))


def row_of(h):
    return slice(h * HEAD, (h + 1) * HEAD)


def in_head(rows):
    shape = (rows, HD)
    lane = lax.broadcasted_iota(jnp.int32, shape, 1)
    low = lax.broadcasted_iota(jnp.int32, shape, 0) * HEAD
    return jnp.logical_and(lane >= low, lane < low + HEAD)


def kernel(
    x_hbm, w_hbm, clip_hbm, og_hbm, att_hbm, ig_hbm,
    xv, wv, clipv, og, feat, ng, inv, dgs, grads, acc, outv, attv, ncol, dcol,
    lsem, send, recv, *rest,
):
    ns, ds_ = rest[:5], rest[5:10]
    bigs = [rest[10 + 7 * i : 17 + 7 * i] for i in range(2 * GROUPS)]
    p = Place()
    barrier = pltpu.get_barrier_semaphore()
    peers = p.peers()
    for peer in peers:
        pl.semaphore_signal(barrier, inc=1, device_id=peer, device_id_type=MESH)

    loads = {
        "clip": pltpu.make_async_copy(clip_hbm, clipv, lsem.at[0]),
        "x": pltpu.make_async_copy(x_hbm.at[0], xv, lsem.at[1]),
        "og": pltpu.make_async_copy(og_hbm.at[0], og, lsem.at[2]),
    }
    for i, (lo, hi) in enumerate(SPANS):
        loads[lo] = pltpu.make_async_copy(w_hbm.at[:, lo:hi], wv.at[:, lo:hi], lsem.at[3 + i])
    for name in ("clip", "x", 1024):
        loads[name].start()

    links = Links(send, recv)
    norm = Small(p, links, ns, False)
    dnorm = Small(p, links, ds_, True)
    state = [Big(p, links, bigs[g], False) for g in range(GROUPS)]
    grad = [Big(p, links, bigs[GROUPS + g], True) for g in range(GROUPS)]

    def project(lo, hi):
        r = tn(wv[:, lo:hi], xv[...])
        pos = min(max(2 * HD - lo, 0), hi - lo)
        if pos:
            feat[lo : lo + pos, :] = jnp.maximum(r[:pos], 0.0).astype(BF16)
        if pos < hi - lo:
            feat[lo + pos : hi, :] = r[pos:].astype(BF16)

    for b in state + grad:
        b.clear()
    loads["clip"].wait()
    is1 = clipv[...] > 0
    m1 = clipv[...].astype(F32)
    m0 = 1.0 - m1
    m0b, m1b = m0.astype(BF16), m1.astype(BF16)

    def split(v, gap=0):
        parts = [v * m0b, v * m1b]
        if gap:
            zero = jnp.zeros((gap, TOK), BF16)
            parts = [parts[0], zero, parts[1], zero]
        return jnp.concatenate(parts, axis=0)

    def put_rows(ref, r):
        ref[...] = jnp.zeros_like(ref)
        for t in range(TILES):
            width = min(WIDE, HD - t * WIDE)
            ref[2 * t : 2 * t + 2, :width] = r[0:2, t * WIDE : t * WIDE + width]

    def get_rows(ref):
        return jnp.concatenate([ref[2 * t : 2 * t + 2, :] for t in range(TILES)], axis=1)

    def columns(ref, dst):
        for t in range(TILES):
            both = ref[2 * t : 2 * t + 2, :]
            both = jnp.concatenate([both, jnp.zeros((6, WIDE), F32)], axis=0)
            dst[t * WIDE : (t + 1) * WIDE, :] = both.T

    def pick(col, h):
        c = col[row_of(h), :]
        return jnp.where(is1, c[:, 1:2], c[:, 0:1])

    def norm_local():
        side = jnp.concatenate([m0b, m1b, jnp.zeros((14, TOK), BF16)], axis=0)
        put_rows(norm.own, nt(side, feat[HD : 2 * HD, :]))

    def state_local(g):
        for i in range(PER):
            h = g * PER + i
            k, v = feat[row_of(HEADS + h), :], feat[row_of(2 * HEADS + h), :]
            state[g].put(i, nt(split(k), v))

    def denominators():
        rows = get_rows(norm.out)[:, :HD]
        keep = in_head(16)
        side = jnp.concatenate(
            [jnp.where(keep, jnp.broadcast_to(rows[c : c + 1], (16, HD)), 0.0) for c in (0, 1)], axis=0
        )
        den = nn(side.astype(BF16), feat[:HD, :])
        inv[...] = 1.0 / (jnp.where(is1, den[16:], den[:16]) + EPS)
        columns(norm.out, ncol)

    def grad_local(g):
        for i in range(PER):
            h = g * PER + i
            v = (og[row_of(h), :].astype(F32) * inv[h : h + 1, :]).astype(BF16)
            ng[row_of(h), :] = v
            grad[g].put(i, nt(split(feat[row_of(h), :]), v))

    def attend(g):
        for i in range(PER):
            h = g * PER + i
            q = feat[row_of(h), :]
            s0, s1 = state[g].pair(i)
            r = inv[h : h + 1, :]
            att = tn(jnp.concatenate([s0, s1], axis=0), split(q))[:HEAD] * r
            attv[row_of(h), :] = att.astype(BF16)
            d = -jnp.sum(og[row_of(h), :].astype(F32) * att, axis=0, keepdims=True) * r
            dgs[h : h + 1, :] = d
            qg = nn(jnp.concatenate([s0, s1], axis=1), split(ng[row_of(h), :], WIDE - HEAD))
            qg = qg + d * pick(ncol, h)
            grads[row_of(h), :] = jnp.where(q.astype(F32) > 0, qg, 0.0).astype(BF16)

    def dnorm_local():
        d = dgs[...]
        both = jnp.concatenate([d * m0, d * m1], axis=0)
        hi = both.astype(BF16)
        lo = (both - hi.astype(F32)).astype(BF16)
        r = nt(jnp.concatenate([hi, lo], axis=0), feat[:HD, :])
        r = r[:32] + r[32:]
        keep = in_head(16)
        rows = [
            jnp.sum(jnp.where(keep, r[16 * c : 16 * c + 16], 0.0), axis=0, keepdims=True) for c in (0, 1)
        ]
        put_rows(dnorm.own, jnp.concatenate(rows, axis=0))

    def value_grads(g):
        for i in range(PER):
            h = g * PER + i
            g0, g1 = grad[g].pair(i)
            r = tn(jnp.concatenate([g0, g1], axis=0), split(feat[row_of(HEADS + h), :]))
            grads[row_of(2 * HEADS + h), :] = r[:HEAD].astype(BF16)

    def key_grads(g):
        for i in range(PER):
            h = g * PER + i
            g0, g1 = grad[g].pair(i)
            v = feat[row_of(2 * HEADS + h), :]
            kg = nn(jnp.concatenate([g0, g1], axis=1), split(v, WIDE - HEAD)) + pick(dcol, h)
            keep = feat[row_of(HEADS + h), :].astype(F32) > 0
            grads[row_of(HEADS + h), :] = jnp.where(keep, kg, 0.0).astype(BF16)

    def back(lo, hi, kind, then=None):
        for m in (0, 1):
            rows = slice(m * HD, (m + 1) * HD)
            r = nn(wv[rows, lo:hi], grads[lo:hi, :])
            if kind > 0:
                r = r + acc[rows, :]
            if kind < 2:
                acc[rows, :] = r
            else:
                outv[rows, :] = r.astype(BF16)
                then(m, rows)

    stores = []

    def store(src, dst, at):
        stores.append(pltpu.make_async_copy(src, dst, lsem.at[at]))
        stores[-1].start()

    loads["x"].wait()
    loads[1024].wait()
    loads[1664].start()
    loads[2304].start()
    project(1024, 1664)
    loads[1664].wait()
    loads[2816].start()
    loads[0].start()
    project(1664, 2304)
    norm_local()
    pl.semaphore_wait(barrier, len(peers))
    norm.s0()
    loads[2304].wait()
    loads[640].start()
    loads["og"].start()
    project(2304, 2816)
    state_local(0)
    state[0].s0()
    loads[2816].wait()
    project(2816, COLS)
    norm.s1()
    state_local(1)
    state[1].s0()
    loads[0].wait()
    project(0, 640)
    state[0].s1()
    loads[640].wait()
    project(640, 1024)
    norm.s2()
    loads["og"].wait()
    denominators()
    grad_local(0)
    grad[0].s0()
    state[1].s1()
    grad_local(1)
    grad[1].s0()
    state[0].s2()
    grad[0].s1()
    state[1].s2()
    grad[1].s1()
    state[0].s3()
    attend(0)
    grad[0].s2()
    state[1].s3()
    attend(1)
    dnorm_local()
    dnorm.s0()
    store(attv, att_hbm.at[0], 0)
    grad[1].s2()
    back(0, 1024, 0)
    dnorm.s1()
    grad[0].s3()
    value_grads(0)
    grad[1].s3()
    value_grads(1)
    back(2304, COLS, 1)
    dnorm.s2()
    columns(dnorm.out, dcol)
    key_grads(0)
    key_grads(1)
    back(1024, 2304, 2, lambda m, rows: store(outv.at[rows, :], ig_hbm.at[0, rows, :], 1 + m))
    links.drain()
    for s in stores:
        s.wait()


def per_device(inputs, weight, clip_of_row, out_grad):
    anywhere = pl.BlockSpec(memory_space=pl.ANY)
    bigs = [r for _ in range(2 * GROUPS) for r in big_scratch()]
    att, grad = pl.pallas_call(
        kernel,
        out_shape=(
            jax.ShapeDtypeStruct((1, HD, TOK), BF16),
            jax.ShapeDtypeStruct((1, D, TOK), BF16),
        ),
        in_specs=[anywhere] * 4,
        out_specs=(anywhere, anywhere),
        scratch_shapes=[
            pltpu.VMEM((D, TOK), BF16),
            pltpu.VMEM((D, COLS), BF16),
            pltpu.VMEM((1, TOK), jnp.int32),
            pltpu.VMEM((HD, TOK), BF16),
            pltpu.VMEM((COLS, TOK), BF16),
            pltpu.VMEM((HD, TOK), BF16),
            pltpu.VMEM((16, TOK), F32),
            pltpu.VMEM((16, TOK), F32),
            pltpu.VMEM((COLS, TOK), BF16),
            pltpu.VMEM((D, TOK), F32),
            pltpu.VMEM((D, TOK), BF16),
            pltpu.VMEM((HD, TOK), BF16),
            pltpu.VMEM((TILES * WIDE, 8), F32),
            pltpu.VMEM((TILES * WIDE, 8), F32),
            pltpu.SemaphoreType.DMA((9,)),
            pltpu.SemaphoreType.DMA((COPIES,)),
            pltpu.SemaphoreType.DMA((COPIES,)),
            *small_scratch(),
            *small_scratch(),
            *bigs,
        ],
        compiler_params=pltpu.CompilerParams(
            collective_id=0, has_side_effects=True, vmem_limit_bytes=67000000
        ),
    )(inputs.swapaxes(1, 2), weight, clip_of_row, out_grad.swapaxes(1, 2))
    return att.swapaxes(1, 2), grad.swapaxes(1, 2)


def solution(mesh):
    placed = (P("frame", "pack", None), P(), P("frame", "pack"), P("frame", "pack", None))
    return jax.shard_map(
        per_device,
        mesh=mesh,
        in_specs=placed,
        out_specs=(P("frame", "pack", None), P("frame", "pack", None)),
        check_vma=False,
    )
```

```python
import jax
import jax.numpy as jnp
from jax import lax
from jax.experimental import pallas as pl
from jax.experimental.pallas import tpu as pltpu
from jax.sharding import PartitionSpec as P

F32 = jnp.float32
BF16 = jnp.bfloat16
MESH = pl.DeviceIdType.MESH
EPS = 1e-06
HEAD = 112
HEADS = 10
WIDE = 128
TOK = 512
D = 2240
HD = HEADS * HEAD
COLS = 3 * HD
RING = 4
PACK = 2 * RING
FRAMES = RING * RING
CHIPS = RING * FRAMES
PIECE = 16
ROWS = CHIPS * PIECE
SPARE = WIDE - HEAD
NROWS = 24
TILES = 9


def tn(a, b):
    return lax.dot_general(a, b, (((0,), (0,)), ((), ())), preferred_element_type=F32)


def nt(a, b):
    return lax.dot_general(a, b, (((1,), (1,)), ((), ())), preferred_element_type=F32)


def nn(a, b):
    return lax.dot_general(a, b, (((1,), (0,)), ((), ())), preferred_element_type=F32)


def row_of(h):
    return slice(h * HEAD, (h + 1) * HEAD)


class Place:
    def __init__(self):
        self.frame = lax.axis_index("frame")
        self.pack = lax.axis_index("pack")
        self.x, self.y = self.frame // RING, self.frame % RING
        self.z, self.c = self.pack // 2, self.pack % 2

    def core_peer(self):
        return self.pack_peer(0)

    def chip(self, e, sign=1):
        dz, dx, dy = e // FRAMES, (e % FRAMES) // RING, e % RING
        x = (self.x + sign * dx + RING) % RING
        y = (self.y + sign * dy + RING) % RING
        return x * RING + y, (self.z + sign * dz + RING) % RING

    def chip_peer(self, e):
        frame, z = self.chip(e)
        return {"frame": frame, "pack": z * 2 + self.c}

    def pack_peer(self, k):
        dz, flip = divmod(k + 1, 2)
        z = (self.z + dz) % RING
        c = (self.c + flip) % 2
        return {"frame": self.frame, "pack": z * 2 + c}

    def frame_peer(self, j):
        return {"frame": (self.frame + j + FRAMES) % FRAMES, "pack": self.pack}

    def peers(self):
        other = [self.pack_peer(k) for k in range(0, PACK - 1, 2)]
        return other + [self.chip_peer(e) for e in range(1, CHIPS)]


class Links:
    def __init__(self, send, recv):
        self.send, self.recv, self.at, self.copies = send, recv, 0, []

    def start(self, src, dst, device, when=None):
        copy = pltpu.make_async_remote_copy(
            src_ref=src,
            dst_ref=dst,
            send_sem=self.send.at[self.at],
            recv_sem=self.recv.at[self.at],
            device_id=device,
            device_id_type=MESH,
        )
        self.at += 1
        if when is None:
            copy.start()
        else:
            pl.when(when)(copy.start)
        self.copies.append((copy, when))
        return copy

    def drain(self):
        for copy, when in self.copies:
            if when is None:
                copy.wait_send()
            else:
                pl.when(when)(copy.wait_send)


class Frames:
    def __init__(self, place, links, reverse):
        self.p, self.l, self.reverse = place, links, reverse

    def spread(self, src, slots):
        f = self.p.frame
        self.w = []
        for j in range(1, FRAMES):
            to, into = (f >= j, f + j < FRAMES) if self.reverse else (f + j < FRAMES, f >= j)
            peer = self.p.frame_peer(-j if self.reverse else j)
            self.w.append((self.l.start(src, slots.at[j - 1], peer, to), into))

    def total(self, own, slots):
        for copy, into in self.w:
            pl.when(into)(copy.wait_recv)
        for j, (_, into) in enumerate(self.w):
            own = own + jnp.where(into, slots[j].astype(F32), 0.0)
        return own


class Small(Frames):
    def __init__(self, place, links, refs, reverse):
        super().__init__(place, links, reverse)
        self.own, self.rz, self.sy, self.ry, self.out = refs

    def s0(self):
        self.wp = [
            self.l.start(self.own, self.rz.at[k], self.p.pack_peer(k)) for k in range(PACK - 1)
        ]

    def s1(self):
        for w in self.wp:
            w.wait_recv()
        total = self.own[...]
        for k in range(PACK - 1):
            total = total + self.rz[k]
        self.sy[...] = total
        self.spread(self.sy, self.ry)

    def s2(self):
        self.out[...] = self.total(self.sy[...], self.ry).astype(BF16).astype(F32)


def lane_of(shape):
    return lax.broadcasted_iota(jnp.int32, shape, 1)


class Big:
    def __init__(self, place, links, refs, sems, reverse):
        self.p, self.l, self.reverse, self.sems = place, links, reverse, sems
        self.acc, self.sc, self.rc, self.sz, self.rz, self.blocks, self.sums, self.out = refs

    def put(self, h, both, last):
        both = jnp.concatenate([both, jnp.zeros((2 * HEAD, SPARE), F32)], axis=1)
        if h < HEAD // SPARE:
            moved = pltpu.roll(last, HEAD - SPARE * h, 1) if SPARE * h < HEAD else last
            both = jnp.where(lane_of(both.shape) < HEAD, both, moved)
        first = self.p.c == 0
        rows = row_of(h)
        self.acc[rows, :] = jnp.where(first, both[:HEAD], both[HEAD:])
        self.sc[rows, :] = jnp.where(first, both[HEAD:], both[:HEAD]).astype(BF16)

    def clear(self):
        rows = slice((HEADS - 1) * HEAD, ROWS)
        self.acc[rows, :] = jnp.zeros((PIECE, WIDE), F32)
        self.sc[rows, :] = jnp.zeros((PIECE, WIDE), BF16)

    def pair(self, h):
        if h < HEADS - 1:
            return self.out[0, row_of(h), :], self.out[1, row_of(h), :]
        found = []
        for c in (0, 1):
            whole = jnp.zeros((HEAD, WIDE), F32)
            lane = lane_of(whole.shape)
            for i in range(HEAD // SPARE):
                part = pltpu.roll(self.out[c, row_of(i), :].astype(F32), SPARE * (i + 1), 1)
                here = jnp.logical_and(lane >= SPARE * i, lane < SPARE * (i + 1))
                whole = jnp.where(here, part, whole)
            found.append(whole.astype(BF16))
        return found

    def piece(self, i):
        return pl.ds(pl.multiple_of(i * PIECE, PIECE), PIECE)

    def mine(self):
        return self.piece(self.p.z * FRAMES + self.p.frame)

    def send(self, at, src, dst, peer):
        pltpu.make_async_remote_copy(
            src_ref=src,
            dst_ref=dst,
            send_sem=self.sems.at[2 * at],
            recv_sem=self.sems.at[2 * at + 1],
            device_id=peer,
            device_id_type=MESH,
        ).start()

    def wait(self, sem):
        most = self.sc.at[0 : ROWS - PIECE, :]
        pltpu.make_async_copy(most, most, self.sems.at[sem]).wait()

    def s0(self):
        self.wp = self.l.start(self.sc, self.rc, self.p.core_peer())

    def s1(self):
        self.wp.wait_recv()
        total = self.acc[...] + self.rc[...].astype(F32)
        self.acc[...] = total
        self.sz[...] = total.astype(BF16)
        for e in range(1, CHIPS):
            frame, z = self.p.chip(e)
            self.send(0, self.sz.at[self.piece(z * FRAMES + frame), :], self.rz.at[e - 1], self.p.chip_peer(e))

    def s2(self):
        self.wait(1)
        for d in range(FRAMES):
            total = self.acc[self.mine(), :] if d == 0 else self.rz[d - 1].astype(F32)
            for dz in range(1, RING):
                total = total + self.rz[dz * FRAMES + d - 1].astype(F32)
            self.blocks[self.p.chip(d, -1)[0]] = total
        total = jnp.zeros((PIECE, WIDE), F32)
        for f in reversed(range(FRAMES)) if self.reverse else range(FRAMES):
            total = total + self.blocks[f]
            self.sums[f] = total.astype(BF16)
        here = self.out.at[self.p.c, self.mine(), :]
        here[...] = self.sums[self.p.frame]
        for e in range(1, CHIPS):
            self.send(1, self.sums.at[self.p.chip(e)[0]], here, self.p.chip_peer(e))

    def s3(self):
        self.wait(3)
        here = self.out.at[self.p.c]
        self.wp = self.l.start(here, here, self.p.core_peer())

    def s4(self):
        self.wp.wait_recv()

    def drain(self):
        self.wait(0)
        self.wait(2)


def small_scratch():
    one = pltpu.VMEM((NROWS, WIDE), F32)
    return [one, pltpu.VMEM((PACK - 1, NROWS, WIDE), F32), one, pltpu.VMEM((FRAMES - 1, NROWS, WIDE), F32), one]


def big_scratch():
    return [
        pltpu.VMEM((ROWS, WIDE), F32),
        pltpu.VMEM((ROWS, WIDE), BF16),
        pltpu.VMEM((ROWS, WIDE), BF16),
        pltpu.VMEM((ROWS, WIDE), BF16),
        pltpu.VMEM((CHIPS - 1, PIECE, WIDE), BF16),
        pltpu.VMEM((FRAMES, PIECE, WIDE), F32),
        pltpu.VMEM((FRAMES, PIECE, WIDE), BF16),
        pltpu.VMEM((2, ROWS, WIDE), BF16),
    ]


COPIES = 2 * (PACK - 1 + FRAMES - 1) + 2 * 2
SPANS = ((1024, 1664), (1664, 2304), (2304, 2816), (2816, COLS), (0, 640), (640, 1024))


def in_head(rows):
    shape = (rows, HD)
    lane = lax.broadcasted_iota(jnp.int32, shape, 1)
    low = lax.broadcasted_iota(jnp.int32, shape, 0) * HEAD
    return jnp.logical_and(lane >= low, lane < low + HEAD)


def kernel(
    x_hbm, w_hbm, clip_hbm, og_hbm, att_hbm, ig_hbm,
    xv, wv, clipv, og, feat, ng, inv, dgs, grads, acc, outv, attv, ncol, dcol,
    lsem, send, recv, ssem, gsem, *rest,
):
    ns, ds_ = rest[:5], rest[5:10]
    bs, bg = rest[10:18], rest[18:26]
    p = Place()
    barrier = pltpu.get_barrier_semaphore()
    peers = p.peers()
    for peer in peers:
        pl.semaphore_signal(barrier, inc=1, device_id=peer, device_id_type=MESH)

    loads = {
        "clip": pltpu.make_async_copy(clip_hbm, clipv, lsem.at[0]),
        "x": pltpu.make_async_copy(x_hbm.at[0], xv, lsem.at[1]),
        "og": pltpu.make_async_copy(og_hbm.at[0], og, lsem.at[2]),
    }
    for i, (lo, hi) in enumerate(SPANS):
        loads[lo] = pltpu.make_async_copy(w_hbm.at[:, lo:hi], wv.at[:, lo:hi], lsem.at[3 + i])
    for name in ("clip", "x", 1024):
        loads[name].start()

    links = Links(send, recv)
    norm = Small(p, links, ns, False)
    dnorm = Small(p, links, ds_, True)
    state = Big(p, links, bs, ssem, False)
    grad = Big(p, links, bg, gsem, True)

    def project(lo, hi):
        r = tn(wv[:, lo:hi], xv[...])
        pos = min(max(2 * HD - lo, 0), hi - lo)
        if pos:
            feat[lo : lo + pos, :] = jnp.maximum(r[:pos], 0.0).astype(BF16)
        if pos < hi - lo:
            feat[lo + pos : hi, :] = r[pos:].astype(BF16)

    for b in (state, grad):
        b.clear()
    loads["clip"].wait()
    is1 = clipv[...] > 0
    m1 = clipv[...].astype(F32)
    m0 = 1.0 - m1
    m0b, m1b = m0.astype(BF16), m1.astype(BF16)

    def split(v, gap=0):
        parts = [v * m0b, v * m1b]
        if gap:
            zero = jnp.zeros((gap, TOK), BF16)
            parts = [parts[0], zero, parts[1], zero]
        return jnp.concatenate(parts, axis=0)

    def put_rows(ref, r):
        ref[...] = jnp.zeros_like(ref)
        for t in range(TILES):
            width = min(WIDE, HD - t * WIDE)
            ref[2 * t : 2 * t + 2, :width] = r[0:2, t * WIDE : t * WIDE + width]

    def get_rows(ref):
        return jnp.concatenate([ref[2 * t : 2 * t + 2, :] for t in range(TILES)], axis=1)

    def columns(ref, dst):
        for t in range(TILES):
            both = ref[2 * t : 2 * t + 2, :]
            both = jnp.concatenate([both, jnp.zeros((6, WIDE), F32)], axis=0)
            dst[t * WIDE : (t + 1) * WIDE, :] = both.T

    def pick(col, h):
        c = col[row_of(h), :]
        return jnp.where(is1, c[:, 1:2], c[:, 0:1])

    def norm_local():
        side = jnp.concatenate([m0b, m1b, jnp.zeros((14, TOK), BF16)], axis=0)
        put_rows(norm.own, nt(side, feat[HD : 2 * HD, :]))

    def put_all(big, terms):
        last = jnp.concatenate([terms(HEADS - 1), jnp.zeros((2 * HEAD, SPARE), F32)], axis=1)
        for h in range(HEADS - 1):
            big.put(h, terms(h), last)

    def state_local():
        put_all(state, lambda h: nt(split(feat[row_of(HEADS + h), :]), feat[row_of(2 * HEADS + h), :]))

    def denominators():
        rows = get_rows(norm.out)[:, :HD]
        keep = in_head(16)
        side = jnp.concatenate(
            [jnp.where(keep, jnp.broadcast_to(rows[c : c + 1], (16, HD)), 0.0) for c in (0, 1)], axis=0
        )
        den = nn(side.astype(BF16), feat[:HD, :])
        inv[...] = 1.0 / (jnp.where(is1, den[16:], den[:16]) + EPS)
        columns(norm.out, ncol)

    def grad_local():
        def terms(h):
            v = (og[row_of(h), :].astype(F32) * inv[h : h + 1, :]).astype(BF16)
            ng[row_of(h), :] = v
            return nt(split(feat[row_of(h), :]), v)

        put_all(grad, terms)

    def attend():
        for h in range(HEADS):
            q = feat[row_of(h), :]
            s0, s1 = state.pair(h)
            r = inv[h : h + 1, :]
            att = tn(jnp.concatenate([s0, s1], axis=0), split(q))[:HEAD] * r
            attv[row_of(h), :] = att.astype(BF16)
            d = -jnp.sum(og[row_of(h), :].astype(F32) * att, axis=0, keepdims=True) * r
            dgs[h : h + 1, :] = d
            qg = nn(jnp.concatenate([s0, s1], axis=1), split(ng[row_of(h), :], WIDE - HEAD))
            qg = qg + d * pick(ncol, h)
            grads[row_of(h), :] = jnp.where(q.astype(F32) > 0, qg, 0.0).astype(BF16)

    def dnorm_local():
        d = dgs[...]
        both = jnp.concatenate([d * m0, d * m1], axis=0)
        hi = both.astype(BF16)
        lo = (both - hi.astype(F32)).astype(BF16)
        r = nt(jnp.concatenate([hi, lo], axis=0), feat[:HD, :])
        r = r[:32] + r[32:]
        keep = in_head(16)
        rows = [
            jnp.sum(jnp.where(keep, r[16 * c : 16 * c + 16], 0.0), axis=0, keepdims=True) for c in (0, 1)
        ]
        put_rows(dnorm.own, jnp.concatenate(rows, axis=0))

    def value_grads():
        for h in range(HEADS):
            g0, g1 = grad.pair(h)
            r = tn(jnp.concatenate([g0, g1], axis=0), split(feat[row_of(HEADS + h), :]))
            grads[row_of(2 * HEADS + h), :] = r[:HEAD].astype(BF16)

    def key_grads():
        for h in range(HEADS):
            g0, g1 = grad.pair(h)
            v = feat[row_of(2 * HEADS + h), :]
            kg = nn(jnp.concatenate([g0, g1], axis=1), split(v, WIDE - HEAD)) + pick(dcol, h)
            keep = feat[row_of(HEADS + h), :].astype(F32) > 0
            grads[row_of(HEADS + h), :] = jnp.where(keep, kg, 0.0).astype(BF16)

    def back(lo, hi, kind, then=None):
        for m in (0, 1):
            rows = slice(m * HD, (m + 1) * HD)
            r = nn(wv[rows, lo:hi], grads[lo:hi, :])
            if kind > 0:
                r = r + acc[rows, :]
            if kind < 2:
                acc[rows, :] = r
            else:
                outv[rows, :] = r.astype(BF16)
                then(m, rows)

    stores = []

    def store(src, dst, at):
        stores.append(pltpu.make_async_copy(src, dst, lsem.at[at]))
        stores[-1].start()

    loads["x"].wait()
    loads[1024].wait()
    loads[1664].start()
    loads[2304].start()
    project(1024, 1664)
    loads[1664].wait()
    loads[2816].start()
    loads[0].start()
    project(1664, 2304)
    norm_local()
    pl.semaphore_wait(barrier, len(peers))
    norm.s0()
    loads[2304].wait()
    loads[640].start()
    loads["og"].start()
    project(2304, 2816)
    loads[2816].wait()
    project(2816, COLS)
    state_local()
    state.s0()
    norm.s1()
    loads[0].wait()
    project(0, 640)
    state.s1()
    loads[640].wait()
    project(640, 1024)
    loads["og"].wait()
    norm.s2()
    denominators()
    grad_local()
    grad.s0()
    state.s2()
    grad.s1()
    state.s3()
    grad.s2()
    state.s4()
    attend()
    dnorm_local()
    dnorm.s0()
    store(attv, att_hbm.at[0], 0)
    back(0, 1024, 0)
    dnorm.s1()
    grad.s3()
    grad.s4()
    value_grads()
    back(2304, COLS, 1)
    dnorm.s2()
    columns(dnorm.out, dcol)
    key_grads()
    back(1024, 2304, 2, lambda m, rows: store(outv.at[rows, :], ig_hbm.at[0, rows, :], 1 + m))
    state.drain()
    grad.drain()
    links.drain()
    for s in stores:
        s.wait()


def per_device(inputs, weight, clip_of_row, out_grad):
    anywhere = pl.BlockSpec(memory_space=pl.ANY)
    att, grad = pl.pallas_call(
        kernel,
        out_shape=(
            jax.ShapeDtypeStruct((1, HD, TOK), BF16),
            jax.ShapeDtypeStruct((1, D, TOK), BF16),
        ),
        in_specs=[anywhere] * 4,
        out_specs=(anywhere, anywhere),
        scratch_shapes=[
            pltpu.VMEM((D, TOK), BF16),
            pltpu.VMEM((D, COLS), BF16),
            pltpu.VMEM((1, TOK), jnp.int32),
            pltpu.VMEM((HD, TOK), BF16),
            pltpu.VMEM((COLS, TOK), BF16),
            pltpu.VMEM((HD, TOK), BF16),
            pltpu.VMEM((16, TOK), F32),
            pltpu.VMEM((16, TOK), F32),
            pltpu.VMEM((COLS, TOK), BF16),
            pltpu.VMEM((D, TOK), F32),
            pltpu.VMEM((D, TOK), BF16),
            pltpu.VMEM((HD, TOK), BF16),
            pltpu.VMEM((TILES * WIDE, 8), F32),
            pltpu.VMEM((TILES * WIDE, 8), F32),
            pltpu.SemaphoreType.DMA((9,)),
            pltpu.SemaphoreType.DMA((COPIES,)),
            pltpu.SemaphoreType.DMA((COPIES,)),
            pltpu.SemaphoreType.DMA((4,)),
            pltpu.SemaphoreType.DMA((4,)),
            *small_scratch(),
            *small_scratch(),
            *big_scratch(),
            *big_scratch(),
        ],
        compiler_params=pltpu.CompilerParams(
            collective_id=0, has_side_effects=True, vmem_limit_bytes=67000000
        ),
    )(inputs.swapaxes(1, 2), weight, clip_of_row, out_grad.swapaxes(1, 2))
    return att.swapaxes(1, 2), grad.swapaxes(1, 2)


def solution(mesh):
    placed = (P("frame", "pack", None), P(), P("frame", "pack"), P("frame", "pack", None))
    return jax.shard_map(
        per_device,
        mesh=mesh,
        in_specs=placed,
        out_specs=(P("frame", "pack", None), P("frame", "pack", None)),
        check_vma=False,
    )
```

```python
import jax
import jax.numpy as jnp
from jax import lax
from jax.experimental import pallas as pl
from jax.experimental.pallas import tpu as pltpu
from jax.sharding import PartitionSpec as P

F32 = jnp.float32
BF16 = jnp.bfloat16
MESH = pl.DeviceIdType.MESH
EPS = 1e-06
HEAD = 112
HEADS = 10
WIDE = 128
TOK = 512
D = 2240
HD = HEADS * HEAD
COLS = 3 * HD
RING = 4
PACK = 2 * RING
FRAMES = RING * RING
CHIPS = RING * FRAMES
PIECE = 16
ROWS = CHIPS * PIECE
SPARE = WIDE - HEAD
NROWS = 24
TILES = 9


def tn(a, b):
    return lax.dot_general(a, b, (((0,), (0,)), ((), ())), preferred_element_type=F32)


def nt(a, b):
    return lax.dot_general(a, b, (((1,), (1,)), ((), ())), preferred_element_type=F32)


def nn(a, b):
    return lax.dot_general(a, b, (((1,), (0,)), ((), ())), preferred_element_type=F32)


def row_of(h):
    return slice(h * HEAD, (h + 1) * HEAD)


def hops(e):
    return sum(min(d, RING - d) for d in (e // FRAMES, (e % FRAMES) // RING, e % RING))


FAR_FIRST = sorted(range(1, CHIPS), key=lambda e: (-hops(e), e))


class Place:
    def __init__(self):
        self.frame = lax.axis_index("frame")
        self.pack = lax.axis_index("pack")
        x, y = lax.div(self.frame, RING), lax.rem(self.frame, RING)
        z, c = lax.div(self.pack, 2), lax.rem(self.pack, 2)
        self.z, self.c = z, c
        self.cs = [c, 1 - c]
        self.zs = [z] + [lax.rem(z + d, RING) for d in range(1, RING)]
        self.ahead = self.grid(x, y, 1)
        self.behind = self.grid(x, y, RING - 1)

    def grid(self, x, y, step):
        xs = [lax.rem(x + step * d, RING) * RING for d in range(RING)]
        ys = [lax.rem(y + step * d, RING) for d in range(RING)]
        return [u + v for u in xs for v in ys]

    def core_peer(self):
        return self.pack_peer(0)

    def chip(self, e):
        return self.ahead[e % FRAMES], self.zs[e // FRAMES]

    def chip_peer(self, e):
        frame, z = self.chip(e)
        return {"frame": frame, "pack": z * 2 + self.c}

    def pack_peer(self, k):
        dz, flip = divmod(k + 1, 2)
        return {"frame": self.frame, "pack": self.zs[dz] * 2 + self.cs[flip]}

    def frame_peer(self, j):
        return {"frame": lax.rem(self.frame + (j % FRAMES), FRAMES), "pack": self.pack}

    def peers(self):
        other = [self.pack_peer(k) for k in range(0, PACK - 1, 2)]
        return other + [self.chip_peer(e) for e in range(1, CHIPS)]


class Links:
    def __init__(self, send, recv):
        self.send, self.recv, self.at, self.copies = send, recv, 0, []

    def start(self, src, dst, device, when=None):
        copy = pltpu.make_async_remote_copy(
            src_ref=src,
            dst_ref=dst,
            send_sem=self.send.at[self.at],
            recv_sem=self.recv.at[self.at],
            device_id=device,
            device_id_type=MESH,
        )
        self.at += 1
        if when is None:
            copy.start()
        else:
            pl.when(when)(copy.start)
        self.copies.append((copy, when))
        return copy

    def drain(self):
        for copy, when in self.copies:
            if when is None:
                copy.wait_send()
            else:
                pl.when(when)(copy.wait_send)


class Frames:
    def __init__(self, place, links, reverse):
        self.p, self.l, self.reverse = place, links, reverse

    def spread(self, src, slots):
        f = self.p.frame
        self.w = []
        for j in range(1, FRAMES):
            to, into = (f >= j, f + j < FRAMES) if self.reverse else (f + j < FRAMES, f >= j)
            peer = self.p.frame_peer(-j if self.reverse else j)
            self.w.append((self.l.start(src, slots.at[j - 1], peer, to), into))

    def total(self, own, slots):
        for copy, into in self.w:
            pl.when(into)(copy.wait_recv)
        for j, (_, into) in enumerate(self.w):
            own = own + jnp.where(into, slots[j].astype(F32), 0.0)
        return own


class Small(Frames):
    def __init__(self, place, links, refs, reverse):
        super().__init__(place, links, reverse)
        self.own, self.rz, self.sy, self.ry, self.out = refs

    def s0(self):
        self.wp = [
            self.l.start(self.own, self.rz.at[k], self.p.pack_peer(k)) for k in range(PACK - 1)
        ]

    def s1(self):
        for w in self.wp:
            w.wait_recv()
        total = self.own[...]
        for k in range(PACK - 1):
            total = total + self.rz[k]
        self.sy[...] = total
        self.spread(self.sy, self.ry)

    def s2(self):
        self.out[...] = self.total(self.sy[...], self.ry).astype(BF16).astype(F32)


def lane_of(shape):
    return lax.broadcasted_iota(jnp.int32, shape, 1)


class Big:
    def __init__(self, place, links, refs, sems, reverse):
        self.p, self.l, self.reverse, self.sems = place, links, reverse, sems
        self.acc, self.sc, self.rc, self.sz, self.rz, self.blocks, self.sums, self.out = refs

    def put(self, h, both, last):
        both = jnp.concatenate([both, jnp.zeros((2 * HEAD, SPARE), F32)], axis=1)
        if h < HEAD // SPARE:
            moved = pltpu.roll(last, HEAD - SPARE * h, 1) if SPARE * h < HEAD else last
            both = jnp.where(lane_of(both.shape) < HEAD, both, moved)
        first = self.p.c == 0
        rows = row_of(h)
        self.acc[rows, :] = jnp.where(first, both[:HEAD], both[HEAD:])
        self.sc[rows, :] = jnp.where(first, both[HEAD:], both[:HEAD]).astype(BF16)

    def clear(self):
        rows = slice((HEADS - 1) * HEAD, ROWS)
        self.acc[rows, :] = jnp.zeros((PIECE, WIDE), F32)
        self.sc[rows, :] = jnp.zeros((PIECE, WIDE), BF16)

    def pair(self, h):
        if h < HEADS - 1:
            return self.out[0, row_of(h), :], self.out[1, row_of(h), :]
        found = []
        for c in (0, 1):
            whole = jnp.zeros((HEAD, WIDE), F32)
            lane = lane_of(whole.shape)
            for i in range(HEAD // SPARE):
                part = pltpu.roll(self.out[c, row_of(i), :].astype(F32), SPARE * (i + 1), 1)
                here = jnp.logical_and(lane >= SPARE * i, lane < SPARE * (i + 1))
                whole = jnp.where(here, part, whole)
            found.append(whole.astype(BF16))
        return found

    def piece(self, i):
        return pl.ds(pl.multiple_of(i * PIECE, PIECE), PIECE)

    def mine(self):
        return self.piece(self.p.z * FRAMES + self.p.frame)

    def send(self, at, src, dst, peer):
        pltpu.make_async_remote_copy(
            src_ref=src,
            dst_ref=dst,
            send_sem=self.sems.at[2 * at],
            recv_sem=self.sems.at[2 * at + 1],
            device_id=peer,
            device_id_type=MESH,
        ).start()

    def wait(self, sem):
        most = self.sc.at[0 : ROWS - PIECE, :]
        pltpu.make_async_copy(most, most, self.sems.at[sem]).wait()

    def s0(self):
        self.wp = self.l.start(self.sc, self.rc, self.p.core_peer())

    def s1(self):
        self.wp.wait_recv()
        total = self.acc[...] + self.rc[...].astype(F32)
        self.acc[...] = total
        self.sz[...] = total.astype(BF16)
        for e in FAR_FIRST:
            frame, z = self.p.chip(e)
            self.send(0, self.sz.at[self.piece(z * FRAMES + frame), :], self.rz.at[e - 1], self.p.chip_peer(e))

    def s2(self):
        self.wait(1)
        for d in range(FRAMES):
            total = self.acc[self.mine(), :] if d == 0 else self.rz[d - 1].astype(F32)
            for dz in range(1, RING):
                total = total + self.rz[dz * FRAMES + d - 1].astype(F32)
            self.blocks[self.p.behind[d]] = total
        total = jnp.zeros((PIECE, WIDE), F32)
        for f in reversed(range(FRAMES)) if self.reverse else range(FRAMES):
            total = total + self.blocks[f]
            self.sums[f] = total.astype(BF16)
        here = self.out.at[self.p.c, self.mine(), :]
        here[...] = self.sums[self.p.frame]
        for e in FAR_FIRST:
            self.send(1, self.sums.at[self.p.chip(e)[0]], here, self.p.chip_peer(e))

    def s3(self):
        self.wait(3)
        here = self.out.at[self.p.c]
        self.wp = self.l.start(here, here, self.p.core_peer())

    def s4(self):
        self.wp.wait_recv()

    def drain(self):
        self.wait(0)
        self.wait(2)


def small_scratch():
    one = pltpu.VMEM((NROWS, WIDE), F32)
    return [one, pltpu.VMEM((PACK - 1, NROWS, WIDE), F32), one, pltpu.VMEM((FRAMES - 1, NROWS, WIDE), F32), one]


def big_scratch():
    return [
        pltpu.VMEM((ROWS, WIDE), F32),
        pltpu.VMEM((ROWS, WIDE), BF16),
        pltpu.VMEM((ROWS, WIDE), BF16),
        pltpu.VMEM((ROWS, WIDE), BF16),
        pltpu.VMEM((CHIPS - 1, PIECE, WIDE), BF16),
        pltpu.VMEM((FRAMES, PIECE, WIDE), F32),
        pltpu.VMEM((FRAMES, PIECE, WIDE), BF16),
        pltpu.VMEM((2, ROWS, WIDE), BF16),
    ]


COPIES = 2 * (PACK - 1 + FRAMES - 1) + 2 * 2
SPANS = ((1024, 1664), (1664, 2304), (2304, 2816), (2816, COLS), (0, 640), (640, 1024))


def in_head(rows):
    shape = (rows, HD)
    lane = lax.broadcasted_iota(jnp.int32, shape, 1)
    low = lax.broadcasted_iota(jnp.int32, shape, 0) * HEAD
    return jnp.logical_and(lane >= low, lane < low + HEAD)


def kernel(
    x_hbm, w_hbm, clip_hbm, og_hbm, attv, outv,
    xv, wv, clipv, og, feat, ng, inv, dgs, grads, acc, ncol, dcol,
    lsem, send, recv, ssem, gsem, *rest,
):
    ns, ds_ = rest[:5], rest[5:10]
    bs, bg = rest[10:18], rest[18:26]
    p = Place()
    barrier = pltpu.get_barrier_semaphore()
    peers = p.peers()
    loads = {
        "clip": pltpu.make_async_copy(clip_hbm, clipv, lsem.at[0]),
        "x": pltpu.make_async_copy(x_hbm.at[0], xv, lsem.at[1]),
        "og": pltpu.make_async_copy(og_hbm.at[0], og, lsem.at[2]),
    }
    for i, (lo, hi) in enumerate(SPANS):
        loads[lo] = pltpu.make_async_copy(w_hbm.at[:, lo:hi], wv.at[:, lo:hi], lsem.at[3 + i])
    for name in ("x", 1024, "clip"):
        loads[name].start()
    for peer in peers:
        pl.semaphore_signal(barrier, inc=1, device_id=peer, device_id_type=MESH)

    links = Links(send, recv)
    norm = Small(p, links, ns, False)
    dnorm = Small(p, links, ds_, True)
    state = Big(p, links, bs, ssem, False)
    grad = Big(p, links, bg, gsem, True)

    def project(lo, hi):
        r = tn(wv[:, lo:hi], xv[...])
        pos = min(max(2 * HD - lo, 0), hi - lo)
        if pos:
            feat[lo : lo + pos, :] = jnp.maximum(r[:pos], 0.0).astype(BF16)
        if pos < hi - lo:
            feat[lo + pos : hi, :] = r[pos:].astype(BF16)

    for b in (state, grad):
        b.clear()
    loads["clip"].wait()
    is1 = clipv[...] > 0
    m1 = clipv[...].astype(F32)
    m0 = 1.0 - m1
    m0b, m1b = m0.astype(BF16), m1.astype(BF16)

    def split(v, gap=0):
        parts = [v * m0b, v * m1b]
        if gap:
            zero = jnp.zeros((gap, TOK), BF16)
            parts = [parts[0], zero, parts[1], zero]
        return jnp.concatenate(parts, axis=0)

    def put_rows(ref, r):
        ref[...] = jnp.zeros_like(ref)
        for t in range(TILES):
            width = min(WIDE, HD - t * WIDE)
            ref[2 * t : 2 * t + 2, :width] = r[0:2, t * WIDE : t * WIDE + width]

    def get_rows(ref):
        return jnp.concatenate([ref[2 * t : 2 * t + 2, :] for t in range(TILES)], axis=1)

    def columns(ref, dst):
        for t in range(TILES):
            both = ref[2 * t : 2 * t + 2, :]
            both = jnp.concatenate([both, jnp.zeros((6, WIDE), F32)], axis=0)
            dst[t * WIDE : (t + 1) * WIDE, :] = both.T

    def pick(col, h):
        c = col[row_of(h), :]
        return jnp.where(is1, c[:, 1:2], c[:, 0:1])

    def norm_local():
        side = jnp.concatenate([m0b, m1b, jnp.zeros((14, TOK), BF16)], axis=0)
        put_rows(norm.own, nt(side, feat[HD : 2 * HD, :]))

    def put_all(big, terms):
        last = jnp.concatenate([terms(HEADS - 1), jnp.zeros((2 * HEAD, SPARE), F32)], axis=1)
        for h in range(HEADS - 1):
            big.put(h, terms(h), last)

    def state_local():
        put_all(state, lambda h: nt(split(feat[row_of(HEADS + h), :]), feat[row_of(2 * HEADS + h), :]))

    def denominators():
        rows = get_rows(norm.out)[:, :HD]
        keep = in_head(16)
        side = jnp.concatenate(
            [jnp.where(keep, jnp.broadcast_to(rows[c : c + 1], (16, HD)), 0.0) for c in (0, 1)], axis=0
        )
        den = nn(side.astype(BF16), feat[:HD, :])
        inv[...] = 1.0 / (jnp.where(is1, den[16:], den[:16]) + EPS)
        columns(norm.out, ncol)

    def grad_local():
        def terms(h):
            v = (og[row_of(h), :].astype(F32) * inv[h : h + 1, :]).astype(BF16)
            ng[row_of(h), :] = v
            return nt(split(feat[row_of(h), :]), v)

        put_all(grad, terms)

    def attend():
        for h in range(HEADS):
            q = feat[row_of(h), :]
            s0, s1 = state.pair(h)
            r = inv[h : h + 1, :]
            att = tn(jnp.concatenate([s0, s1], axis=0), split(q))[:HEAD] * r
            attv[0, row_of(h), :] = att.astype(BF16)
            d = -jnp.sum(og[row_of(h), :].astype(F32) * att, axis=0, keepdims=True) * r
            dgs[h : h + 1, :] = d
            qg = nn(jnp.concatenate([s0, s1], axis=1), split(ng[row_of(h), :], WIDE - HEAD))
            qg = qg + d * pick(ncol, h)
            grads[row_of(h), :] = jnp.where(q.astype(F32) > 0, qg, 0.0).astype(BF16)

    def dnorm_local():
        d = dgs[...]
        both = jnp.concatenate([d * m0, d * m1], axis=0)
        hi = both.astype(BF16)
        lo = (both - hi.astype(F32)).astype(BF16)
        r = nt(jnp.concatenate([hi, lo], axis=0), feat[:HD, :])
        r = r[:32] + r[32:]
        keep = in_head(16)
        rows = [
            jnp.sum(jnp.where(keep, r[16 * c : 16 * c + 16], 0.0), axis=0, keepdims=True) for c in (0, 1)
        ]
        put_rows(dnorm.own, jnp.concatenate(rows, axis=0))

    def value_grads():
        for h in range(HEADS):
            g0, g1 = grad.pair(h)
            r = tn(jnp.concatenate([g0, g1], axis=0), split(feat[row_of(HEADS + h), :]))
            grads[row_of(2 * HEADS + h), :] = r[:HEAD].astype(BF16)

    def key_grads():
        for h in range(HEADS):
            g0, g1 = grad.pair(h)
            v = feat[row_of(2 * HEADS + h), :]
            kg = nn(jnp.concatenate([g0, g1], axis=1), split(v, WIDE - HEAD)) + pick(dcol, h)
            keep = feat[row_of(HEADS + h), :].astype(F32) > 0
            grads[row_of(HEADS + h), :] = jnp.where(keep, kg, 0.0).astype(BF16)

    def back(lo, hi, kind):
        for m in (0, 1):
            rows = slice(m * HD, (m + 1) * HD)
            r = nn(wv[rows, lo:hi], grads[lo:hi, :])
            if kind > 0:
                r = r + acc[rows, :]
            if kind < 2:
                acc[rows, :] = r
            else:
                outv[0, rows, :] = r.astype(BF16)

    loads["x"].wait()
    loads[1024].wait()
    loads[1664].start()
    loads[2304].start()
    project(1024, 1664)
    loads[1664].wait()
    loads[2816].start()
    loads[0].start()
    project(1664, 2304)
    norm_local()
    pl.semaphore_wait(barrier, len(peers))
    norm.s0()
    loads[2304].wait()
    loads[640].start()
    loads["og"].start()
    project(2304, 2816)
    loads[2816].wait()
    project(2816, COLS)
    norm.s1()
    state_local()
    state.s0()
    loads[0].wait()
    project(0, 256)
    state.s1()
    project(256, 640)
    loads[640].wait()
    project(640, 1024)
    loads["og"].wait()
    norm.s2()
    denominators()
    grad_local()
    grad.s0()
    state.s2()
    grad.s1()
    state.s3()
    grad.s2()
    state.s4()
    attend()
    dnorm_local()
    dnorm.s0()
    back(0, 1024, 0)
    dnorm.s1()
    grad.s3()
    grad.s4()
    value_grads()
    back(2304, COLS, 1)
    dnorm.s2()
    columns(dnorm.out, dcol)
    key_grads()
    back(1024, 2304, 2)
    state.drain()
    grad.drain()
    links.drain()


def per_device(inputs, weight, clip_of_row, out_grad):
    anywhere = pl.BlockSpec(memory_space=pl.ANY)
    att, grad = pl.pallas_call(
        kernel,
        out_shape=(pltpu.VMEM((1, HD, TOK), BF16), pltpu.VMEM((1, D, TOK), BF16)),
        in_specs=[anywhere] * 4,
        out_specs=(pl.BlockSpec(memory_space=pltpu.VMEM),) * 2,
        scratch_shapes=[
            pltpu.VMEM((D, TOK), BF16),
            pltpu.VMEM((D, COLS), BF16),
            pltpu.VMEM((1, TOK), jnp.int32),
            pltpu.VMEM((HD, TOK), BF16),
            pltpu.VMEM((COLS, TOK), BF16),
            pltpu.VMEM((HD, TOK), BF16),
            pltpu.VMEM((16, TOK), F32),
            pltpu.VMEM((16, TOK), F32),
            pltpu.VMEM((COLS, TOK), BF16),
            pltpu.VMEM((D, TOK), F32),
            pltpu.VMEM((TILES * WIDE, 8), F32),
            pltpu.VMEM((TILES * WIDE, 8), F32),
            pltpu.SemaphoreType.DMA((9,)),
            pltpu.SemaphoreType.DMA((COPIES,)),
            pltpu.SemaphoreType.DMA((COPIES,)),
            pltpu.SemaphoreType.DMA((4,)),
            pltpu.SemaphoreType.DMA((4,)),
            *small_scratch(),
            *small_scratch(),
            *big_scratch(),
            *big_scratch(),
        ],
        compiler_params=pltpu.CompilerParams(
            collective_id=0, has_side_effects=True, vmem_limit_bytes=54000000
        ),
    )(inputs.swapaxes(1, 2), weight, clip_of_row, out_grad.swapaxes(1, 2))
    return att.swapaxes(1, 2), grad.swapaxes(1, 2)


def solution(mesh):
    placed = (P("frame", "pack", None), P(), P("frame", "pack"), P("frame", "pack", None))
    return jax.shard_map(
        per_device,
        mesh=mesh,
        in_specs=placed,
        out_specs=(P("frame", "pack", None), P("frame", "pack", None)),
        check_vma=False,
    )
```

```python
import jax
import jax.numpy as jnp
from jax import lax
from jax.experimental import pallas as pl
from jax.experimental.pallas import tpu as pltpu
from jax.sharding import PartitionSpec as P

F32 = jnp.float32
BF16 = jnp.bfloat16
MESH = pl.DeviceIdType.MESH
EPS = 1e-06
HEAD = 112
HEADS = 10
WIDE = 128
TOK = 512
D = 2240
HD = HEADS * HEAD
COLS = 3 * HD
RING = 4
PACK = 2 * RING
FRAMES = RING * RING
CHIPS = RING * FRAMES
PIECE = 16
ROWS = CHIPS * PIECE
SPARE = WIDE - HEAD
NROWS = 24
TILES = 9


def tn(a, b):
    return lax.dot_general(a, b, (((0,), (0,)), ((), ())), preferred_element_type=F32)


def nt(a, b):
    return lax.dot_general(a, b, (((1,), (1,)), ((), ())), preferred_element_type=F32)


def nn(a, b):
    return lax.dot_general(a, b, (((1,), (0,)), ((), ())), preferred_element_type=F32)


def row_of(h):
    return slice(h * HEAD, (h + 1) * HEAD)


def hops(e):
    return sum(min(d, RING - d) for d in (e // FRAMES, (e % FRAMES) // RING, e % RING))


FAR_FIRST = sorted(range(1, CHIPS), key=lambda e: (-hops(e), e))


class Place:
    def __init__(self):
        self.frame = lax.axis_index("frame")
        self.pack = lax.axis_index("pack")
        x, y = lax.div(self.frame, RING), lax.rem(self.frame, RING)
        z, c = lax.div(self.pack, 2), lax.rem(self.pack, 2)
        self.z, self.c = z, c
        self.cs = [c, 1 - c]
        self.zs = [z] + [lax.rem(z + d, RING) for d in range(1, RING)]
        self.ahead = self.grid(x, y, 1)
        self.behind = self.grid(x, y, RING - 1)

    def grid(self, x, y, step):
        xs = [lax.rem(x + step * d, RING) * RING for d in range(RING)]
        ys = [lax.rem(y + step * d, RING) for d in range(RING)]
        return [u + v for u in xs for v in ys]

    def core_peer(self):
        return self.pack_peer(0)

    def chip(self, e):
        return self.ahead[e % FRAMES], self.zs[e // FRAMES]

    def chip_peer(self, e):
        frame, z = self.chip(e)
        return {"frame": frame, "pack": z * 2 + self.c}

    def pack_peer(self, k):
        dz, flip = divmod(k + 1, 2)
        return {"frame": self.frame, "pack": self.zs[dz] * 2 + self.cs[flip]}

    def frame_peer(self, j):
        return {"frame": lax.rem(self.frame + (j % FRAMES), FRAMES), "pack": self.pack}

    def peers(self):
        return [self.pack_peer(k) for k in range(PACK - 1)] + self.frame_peers()

    def frame_peers(self):
        return [self.frame_peer(j) for j in range(1, FRAMES)]


class Links:
    def __init__(self, send, recv):
        self.send, self.recv, self.at, self.copies = send, recv, 0, []

    def start(self, src, dst, device, when=None):
        copy = pltpu.make_async_remote_copy(
            src_ref=src,
            dst_ref=dst,
            send_sem=self.send.at[self.at],
            recv_sem=self.recv.at[self.at],
            device_id=device,
            device_id_type=MESH,
        )
        self.at += 1
        if when is None:
            copy.start()
        else:
            pl.when(when)(copy.start)
        self.copies.append((copy, when))
        return copy

    def drain(self):
        for copy, when in self.copies:
            if when is None:
                copy.wait_send()
            else:
                pl.when(when)(copy.wait_send)


class Frames:
    def __init__(self, place, links, reverse):
        self.p, self.l, self.reverse = place, links, reverse

    def spread(self, src, slots):
        f = self.p.frame
        self.w = []
        for j in range(1, FRAMES):
            to, into = (f >= j, f + j < FRAMES) if self.reverse else (f + j < FRAMES, f >= j)
            peer = self.p.frame_peer(-j if self.reverse else j)
            self.w.append((self.l.start(src, slots.at[j - 1], peer, to), into))

    def total(self, own, slots):
        for copy, into in self.w:
            pl.when(into)(copy.wait_recv)
        for j, (_, into) in enumerate(self.w):
            own = own + jnp.where(into, slots[j].astype(F32), 0.0)
        return own


class Small(Frames):
    def __init__(self, place, links, refs, reverse):
        super().__init__(place, links, reverse)
        self.own, self.rz, self.sy, self.ry, self.out = refs

    def s0(self):
        self.wp = [
            self.l.start(self.own, self.rz.at[k], self.p.pack_peer(k)) for k in range(PACK - 1)
        ]

    def s1(self):
        for w in self.wp:
            w.wait_recv()
        total = self.own[...]
        for k in range(PACK - 1):
            total = total + self.rz[k]
        self.sy[...] = total
        self.spread(self.sy, self.ry)

    def s2(self):
        self.out[...] = self.total(self.sy[...], self.ry).astype(BF16).astype(F32)


def lane_of(shape):
    return lax.broadcasted_iota(jnp.int32, shape, 1)


class Big:
    def __init__(self, place, links, refs, sems, reverse):
        self.p, self.l, self.reverse, self.sems = place, links, reverse, sems
        self.acc, self.sc, self.rc, self.sz, self.rz, self.blocks, self.sums, self.out = refs

    def put(self, h, both, last):
        both = jnp.concatenate([both, jnp.zeros((2 * HEAD, SPARE), F32)], axis=1)
        if h < HEAD // SPARE:
            moved = pltpu.roll(last, HEAD - SPARE * h, 1) if SPARE * h < HEAD else last
            both = jnp.where(lane_of(both.shape) < HEAD, both, moved)
        first = self.p.c == 0
        rows = row_of(h)
        self.acc[rows, :] = jnp.where(first, both[:HEAD], both[HEAD:])
        self.sc[rows, :] = jnp.where(first, both[HEAD:], both[:HEAD]).astype(BF16)

    def clear(self):
        rows = slice((HEADS - 1) * HEAD, ROWS)
        self.acc[rows, :] = jnp.zeros((PIECE, WIDE), F32)
        self.sc[rows, :] = jnp.zeros((PIECE, WIDE), BF16)

    def pair(self, h):
        if h < HEADS - 1:
            return self.out[0, row_of(h), :], self.out[1, row_of(h), :]
        found = []
        for c in (0, 1):
            whole = jnp.zeros((HEAD, WIDE), F32)
            lane = lane_of(whole.shape)
            for i in range(HEAD // SPARE):
                part = pltpu.roll(self.out[c, row_of(i), :].astype(F32), SPARE * (i + 1), 1)
                here = jnp.logical_and(lane >= SPARE * i, lane < SPARE * (i + 1))
                whole = jnp.where(here, part, whole)
            found.append(whole.astype(BF16))
        return found

    def piece(self, i):
        return pl.ds(pl.multiple_of(i * PIECE, PIECE), PIECE)

    def mine(self):
        return self.piece(self.p.z * FRAMES + self.p.frame)

    def send(self, at, src, dst, peer):
        pltpu.make_async_remote_copy(
            src_ref=src,
            dst_ref=dst,
            send_sem=self.sems.at[2 * at],
            recv_sem=self.sems.at[2 * at + 1],
            device_id=peer,
            device_id_type=MESH,
        ).start()

    def wait(self, sem):
        most = self.sc.at[0 : ROWS - PIECE, :]
        pltpu.make_async_copy(most, most, self.sems.at[sem]).wait()

    def s0(self):
        self.wp = self.l.start(self.sc, self.rc, self.p.core_peer())

    def s1(self):
        self.wp.wait_recv()
        total = self.acc[...] + self.rc[...].astype(F32)
        self.acc[...] = total
        self.sz[...] = total.astype(BF16)
        for e in FAR_FIRST:
            frame, z = self.p.chip(e)
            self.send(0, self.sz.at[self.piece(z * FRAMES + frame), :], self.rz.at[e - 1], self.p.chip_peer(e))

    def s2(self):
        self.wait(1)
        for d in range(FRAMES):
            total = self.acc[self.mine(), :] if d == 0 else self.rz[d - 1].astype(F32)
            for dz in range(1, RING):
                total = total + self.rz[dz * FRAMES + d - 1].astype(F32)
            self.blocks[self.p.behind[d]] = total
        total = jnp.zeros((PIECE, WIDE), F32)
        for f in reversed(range(FRAMES)) if self.reverse else range(FRAMES):
            total = total + self.blocks[f]
            self.sums[f] = total.astype(BF16)
        here = self.out.at[self.p.c, self.mine(), :]
        here[...] = self.sums[self.p.frame]
        for e in FAR_FIRST:
            self.send(1, self.sums.at[self.p.chip(e)[0]], here, self.p.chip_peer(e))

    def s3(self):
        self.wait(3)
        here = self.out.at[self.p.c]
        self.wp = self.l.start(here, here, self.p.core_peer())

    def s4(self):
        self.wp.wait_recv()

    def drain(self):
        self.wait(0)
        self.wait(2)


def small_scratch():
    one = pltpu.VMEM((NROWS, WIDE), F32)
    return [one, pltpu.VMEM((PACK - 1, NROWS, WIDE), F32), one, pltpu.VMEM((FRAMES - 1, NROWS, WIDE), F32), one]


def big_scratch():
    return [
        pltpu.VMEM((ROWS, WIDE), F32),
        pltpu.VMEM((ROWS, WIDE), BF16),
        pltpu.VMEM((ROWS, WIDE), BF16),
        pltpu.VMEM((ROWS, WIDE), BF16),
        pltpu.VMEM((CHIPS - 1, PIECE, WIDE), BF16),
        pltpu.VMEM((FRAMES, PIECE, WIDE), F32),
        pltpu.VMEM((FRAMES, PIECE, WIDE), BF16),
        pltpu.VMEM((2, ROWS, WIDE), BF16),
    ]


COPIES = 2 * (PACK - 1 + FRAMES - 1) + 2 * 2
SPANS = ((1024, 1664), (1664, 2304), (2304, 2816), (2816, COLS), (0, 640), (640, 1024))


def in_head(rows):
    shape = (rows, HD)
    lane = lax.broadcasted_iota(jnp.int32, shape, 1)
    low = lax.broadcasted_iota(jnp.int32, shape, 0) * HEAD
    return jnp.logical_and(lane >= low, lane < low + HEAD)


def kernel(
    x_hbm, w_hbm, clip_hbm, og_hbm, attv, outv,
    xv, wv, clipv, og, feat, ng, inv, dgs, grads, acc, ncol, dcol,
    lsem, send, recv, ssem, gsem, entry, *rest,
):
    ns, ds_ = rest[:5], rest[5:10]
    bs, bg = rest[10:18], rest[18:26]
    p = Place()
    barrier = pltpu.get_barrier_semaphore()
    peers = p.peers()
    loads = {
        "clip": pltpu.make_async_copy(clip_hbm, clipv, lsem.at[0]),
        "x": pltpu.make_async_copy(x_hbm.at[0], xv, lsem.at[1]),
        "og": pltpu.make_async_copy(og_hbm.at[0], og, lsem.at[2]),
    }
    for i, (lo, hi) in enumerate(SPANS):
        loads[lo] = pltpu.make_async_copy(w_hbm.at[:, lo:hi], wv.at[:, lo:hi], lsem.at[3 + i])
    for name in ("x", 1024, "clip"):
        loads[name].start()
    for peer in peers:
        pl.semaphore_signal(barrier, inc=1, device_id=peer, device_id_type=MESH)

    links = Links(send, recv)
    norm = Small(p, links, ns, False)
    dnorm = Small(p, links, ds_, True)
    state = Big(p, links, bs, ssem, False)
    grad = Big(p, links, bg, gsem, True)

    def project(lo, hi):
        r = tn(wv[:, lo:hi], xv[...])
        pos = min(max(2 * HD - lo, 0), hi - lo)
        if pos:
            feat[lo : lo + pos, :] = jnp.maximum(r[:pos], 0.0).astype(BF16)
        if pos < hi - lo:
            feat[lo + pos : hi, :] = r[pos:].astype(BF16)

    for b in (state, grad):
        b.clear()
    loads["clip"].wait()
    is1 = clipv[...] > 0
    m1 = clipv[...].astype(F32)
    m0 = 1.0 - m1
    m0b, m1b = m0.astype(BF16), m1.astype(BF16)

    def split(v, gap=0):
        parts = [v * m0b, v * m1b]
        if gap:
            zero = jnp.zeros((gap, TOK), BF16)
            parts = [parts[0], zero, parts[1], zero]
        return jnp.concatenate(parts, axis=0)

    def put_rows(ref, r):
        ref[...] = jnp.zeros_like(ref)
        for t in range(TILES):
            width = min(WIDE, HD - t * WIDE)
            ref[2 * t : 2 * t + 2, :width] = r[0:2, t * WIDE : t * WIDE + width]

    def get_rows(ref):
        return jnp.concatenate([ref[2 * t : 2 * t + 2, :] for t in range(TILES)], axis=1)

    def columns(ref, dst):
        for t in range(TILES):
            both = ref[2 * t : 2 * t + 2, :]
            both = jnp.concatenate([both, jnp.zeros((6, WIDE), F32)], axis=0)
            dst[t * WIDE : (t + 1) * WIDE, :] = both.T

    def pick(col, h):
        c = col[row_of(h), :]
        return jnp.where(is1, c[:, 1:2], c[:, 0:1])

    def norm_local():
        side = jnp.concatenate([m0b, m1b, jnp.zeros((14, TOK), BF16)], axis=0)
        put_rows(norm.own, nt(side, feat[HD : 2 * HD, :]))

    def put_all(big, terms):
        last = jnp.concatenate([terms(HEADS - 1), jnp.zeros((2 * HEAD, SPARE), F32)], axis=1)
        for h in range(HEADS - 1):
            big.put(h, terms(h), last)

    def state_local():
        put_all(state, lambda h: nt(split(feat[row_of(HEADS + h), :]), feat[row_of(2 * HEADS + h), :]))

    def denominators():
        rows = get_rows(norm.out)[:, :HD]
        keep = in_head(16)
        side = jnp.concatenate(
            [jnp.where(keep, jnp.broadcast_to(rows[c : c + 1], (16, HD)), 0.0) for c in (0, 1)], axis=0
        )
        den = nn(side.astype(BF16), feat[:HD, :])
        inv[...] = 1.0 / (jnp.where(is1, den[16:], den[:16]) + EPS)
        columns(norm.out, ncol)

    def grad_local():
        def terms(h):
            v = (og[row_of(h), :].astype(F32) * inv[h : h + 1, :]).astype(BF16)
            ng[row_of(h), :] = v
            return nt(split(feat[row_of(h), :]), v)

        put_all(grad, terms)

    def attend():
        for h in range(HEADS):
            q = feat[row_of(h), :]
            s0, s1 = state.pair(h)
            r = inv[h : h + 1, :]
            att = tn(jnp.concatenate([s0, s1], axis=0), split(q))[:HEAD] * r
            attv[0, row_of(h), :] = att.astype(BF16)
            d = -jnp.sum(og[row_of(h), :].astype(F32) * att, axis=0, keepdims=True) * r
            dgs[h : h + 1, :] = d
            qg = nn(jnp.concatenate([s0, s1], axis=1), split(ng[row_of(h), :], WIDE - HEAD))
            qg = qg + d * pick(ncol, h)
            grads[row_of(h), :] = jnp.where(q.astype(F32) > 0, qg, 0.0).astype(BF16)

    def dnorm_local():
        d = dgs[...]
        both = jnp.concatenate([d * m0, d * m1], axis=0)
        hi = both.astype(BF16)
        lo = (both - hi.astype(F32)).astype(BF16)
        r = nt(jnp.concatenate([hi, lo], axis=0), feat[:HD, :])
        r = r[:32] + r[32:]
        keep = in_head(16)
        rows = [
            jnp.sum(jnp.where(keep, r[16 * c : 16 * c + 16], 0.0), axis=0, keepdims=True) for c in (0, 1)
        ]
        put_rows(dnorm.own, jnp.concatenate(rows, axis=0))

    def value_grads():
        for h in range(HEADS):
            g0, g1 = grad.pair(h)
            r = tn(jnp.concatenate([g0, g1], axis=0), split(feat[row_of(HEADS + h), :]))
            grads[row_of(2 * HEADS + h), :] = r[:HEAD].astype(BF16)

    def key_grads():
        for h in range(HEADS):
            g0, g1 = grad.pair(h)
            v = feat[row_of(2 * HEADS + h), :]
            kg = nn(jnp.concatenate([g0, g1], axis=1), split(v, WIDE - HEAD)) + pick(dcol, h)
            keep = feat[row_of(HEADS + h), :].astype(F32) > 0
            grads[row_of(HEADS + h), :] = jnp.where(keep, kg, 0.0).astype(BF16)

    def back(lo, hi, kind):
        for m in (0, 1):
            rows = slice(m * HD, (m + 1) * HD)
            r = nn(wv[rows, lo:hi], grads[lo:hi, :])
            if kind > 0:
                r = r + acc[rows, :]
            if kind < 2:
                acc[rows, :] = r
            else:
                outv[0, rows, :] = r.astype(BF16)

    loads["x"].wait()
    loads[1024].wait()
    loads[1664].start()
    loads[2304].start()
    project(1024, 1664)
    loads[1664].wait()
    loads[2816].start()
    loads[0].start()
    project(1664, 2304)
    norm_local()
    pl.semaphore_wait(barrier, len(peers))
    norm.s0()
    for peer in p.frame_peers():
        pl.semaphore_signal(entry, inc=1, device_id=peer, device_id_type=MESH)
    loads[2304].wait()
    loads[640].start()
    loads["og"].start()
    project(2304, 2816)
    loads[2816].wait()
    project(2816, COLS)
    norm.s1()
    state_local()
    state.s0()
    loads[0].wait()
    project(0, 256)
    pl.semaphore_wait(entry, FRAMES - 1)
    state.s1()
    project(256, 640)
    loads[640].wait()
    project(640, 1024)
    loads["og"].wait()
    norm.s2()
    denominators()
    grad_local()
    grad.s0()
    grad.s1()
    state.s2()
    grad.s2()
    state.s3()
    state.s4()
    attend()
    dnorm_local()
    dnorm.s0()
    back(0, 1024, 0)
    grad.s3()
    dnorm.s1()
    grad.s4()
    value_grads()
    back(2304, COLS, 1)
    dnorm.s2()
    columns(dnorm.out, dcol)
    key_grads()
    back(1024, 2304, 2)
    state.drain()
    grad.drain()
    links.drain()


def per_device(inputs, weight, clip_of_row, out_grad):
    anywhere = pl.BlockSpec(memory_space=pl.ANY)
    att, grad = pl.pallas_call(
        kernel,
        out_shape=(pltpu.VMEM((1, HD, TOK), BF16), pltpu.VMEM((1, D, TOK), BF16)),
        in_specs=[anywhere] * 4,
        out_specs=(pl.BlockSpec(memory_space=pltpu.VMEM),) * 2,
        scratch_shapes=[
            pltpu.VMEM((D, TOK), BF16),
            pltpu.VMEM((D, COLS), BF16),
            pltpu.VMEM((1, TOK), jnp.int32),
            pltpu.VMEM((HD, TOK), BF16),
            pltpu.VMEM((COLS, TOK), BF16),
            pltpu.VMEM((HD, TOK), BF16),
            pltpu.VMEM((16, TOK), F32),
            pltpu.VMEM((16, TOK), F32),
            pltpu.VMEM((COLS, TOK), BF16),
            pltpu.VMEM((D, TOK), F32),
            pltpu.VMEM((TILES * WIDE, 8), F32),
            pltpu.VMEM((TILES * WIDE, 8), F32),
            pltpu.SemaphoreType.DMA((9,)),
            pltpu.SemaphoreType.DMA((COPIES,)),
            pltpu.SemaphoreType.DMA((COPIES,)),
            pltpu.SemaphoreType.DMA((4,)),
            pltpu.SemaphoreType.DMA((4,)),
            pltpu.SemaphoreType.REGULAR,
            *small_scratch(),
            *small_scratch(),
            *big_scratch(),
            *big_scratch(),
        ],
        compiler_params=pltpu.CompilerParams(
            collective_id=0, has_side_effects=True, vmem_limit_bytes=54000000
        ),
    )(inputs.swapaxes(1, 2), weight, clip_of_row, out_grad.swapaxes(1, 2))
    return att.swapaxes(1, 2), grad.swapaxes(1, 2)


def solution(mesh):
    placed = (P("frame", "pack", None), P(), P("frame", "pack"), P("frame", "pack", None))
    return jax.shard_map(
        per_device,
        mesh=mesh,
        in_specs=placed,
        out_specs=(P("frame", "pack", None), P("frame", "pack", None)),
        check_vma=False,
    )
```

```python
import jax
import jax.numpy as jnp
from jax import lax
from jax.experimental import pallas as pl
from jax.experimental.pallas import tpu as pltpu
from jax.sharding import PartitionSpec as P

F32 = jnp.float32
BF16 = jnp.bfloat16
MESH = pl.DeviceIdType.MESH
EPS = 1e-06
HEAD = 112
HEADS = 10
WIDE = 128
TOK = 512
D = 2240
HD = HEADS * HEAD
COLS = 3 * HD
RING = 4
PACK = 2 * RING
FRAMES = RING * RING
CHIPS = RING * FRAMES
PIECE = 16
ROWS = CHIPS * PIECE
SPARE = WIDE - HEAD
NROWS = 24
TILES = 9


def tn(a, b):
    return lax.dot_general(a, b, (((0,), (0,)), ((), ())), preferred_element_type=F32)


def nt(a, b):
    return lax.dot_general(a, b, (((1,), (1,)), ((), ())), preferred_element_type=F32)


def nn(a, b):
    return lax.dot_general(a, b, (((1,), (0,)), ((), ())), preferred_element_type=F32)


def row_of(h):
    return slice(h * HEAD, (h + 1) * HEAD)


def hops(e):
    return sum(min(d, RING - d) for d in (e // FRAMES, (e % FRAMES) // RING, e % RING))


FAR_FIRST = sorted(range(1, CHIPS), key=lambda e: (-hops(e), e))


class Place:
    def __init__(self):
        self.frame = lax.axis_index("frame")
        self.pack = lax.axis_index("pack")
        x, y = lax.div(self.frame, RING), lax.rem(self.frame, RING)
        z, c = lax.div(self.pack, 2), lax.rem(self.pack, 2)
        self.z, self.c = z, c
        self.cs = [c, 1 - c]
        self.zs = [z] + [lax.rem(z + d, RING) for d in range(1, RING)]
        self.ahead = self.grid(x, y, 1)
        self.behind = self.grid(x, y, RING - 1)

    def grid(self, x, y, step):
        xs = [lax.rem(x + step * d, RING) * RING for d in range(RING)]
        ys = [lax.rem(y + step * d, RING) for d in range(RING)]
        return [u + v for u in xs for v in ys]

    def core_peer(self):
        return self.pack_peer(0)

    def chip(self, e):
        return self.ahead[e % FRAMES], self.zs[e // FRAMES]

    def chip_peer(self, e):
        frame, z = self.chip(e)
        return {"frame": frame, "pack": z * 2 + self.c}

    def pack_peer(self, k):
        dz, flip = divmod(k + 1, 2)
        return {"frame": self.frame, "pack": self.zs[dz] * 2 + self.cs[flip]}

    def frame_peer(self, j):
        return {"frame": lax.rem(self.frame + (j % FRAMES), FRAMES), "pack": self.pack}

    def peers(self):
        return [self.pack_peer(k) for k in range(PACK - 1)] + self.frame_peers()

    def frame_peers(self):
        return [self.frame_peer(j) for j in range(1, FRAMES)]


class Links:
    def __init__(self, send, recv):
        self.send, self.recv, self.at, self.copies = send, recv, 0, []

    def start(self, src, dst, device, when=None):
        copy = pltpu.make_async_remote_copy(
            src_ref=src,
            dst_ref=dst,
            send_sem=self.send.at[self.at],
            recv_sem=self.recv.at[self.at],
            device_id=device,
            device_id_type=MESH,
        )
        self.at += 1
        if when is None:
            copy.start()
        else:
            pl.when(when)(copy.start)
        self.copies.append((copy, when))
        return copy

    def drain(self):
        for copy, when in self.copies:
            if when is None:
                copy.wait_send()
            else:
                pl.when(when)(copy.wait_send)


class Frames:
    def __init__(self, place, links, reverse):
        self.p, self.l, self.reverse = place, links, reverse

    def spread(self, src, slots):
        f = self.p.frame
        self.w = []
        for j in sorted(range(1, FRAMES), key=lambda j: (-hops(j), j)):
            to, into = (f >= j, f + j < FRAMES) if self.reverse else (f + j < FRAMES, f >= j)
            peer = self.p.frame_peer(-j if self.reverse else j)
            self.w.append((self.l.start(src, slots.at[j - 1], peer, to), into, j - 1))

    def total(self, own, slots):
        for copy, into, _ in self.w:
            pl.when(into)(copy.wait_recv)
        for _, into, slot in self.w:
            own = own + jnp.where(into, slots[slot], 0.0)
        return own


class Small(Frames):
    def __init__(self, place, links, refs, reverse):
        super().__init__(place, links, reverse)
        self.own, self.rz, self.sy, self.ry, self.out = refs

    def s0(self):
        self.wp = [
            self.l.start(self.own, self.rz.at[k], self.p.pack_peer(k)) for k in range(PACK - 1)
        ]

    def s1(self):
        for w in self.wp:
            w.wait_recv()
        total = self.own[...]
        for k in range(PACK - 1):
            total = total + self.rz[k]
        self.sy[...] = total
        self.spread(self.sy, self.ry)

    def s2(self):
        self.out[...] = self.total(self.sy[...], self.ry).astype(BF16).astype(F32)


def lane_of(shape):
    return lax.broadcasted_iota(jnp.int32, shape, 1)


class Big:
    def __init__(self, place, links, refs, sems, reverse):
        self.p, self.l, self.reverse, self.sems = place, links, reverse, sems
        self.acc, self.sc, self.rc, self.sz, self.rz, self.blocks, self.sums, self.out = refs

    def put(self, h, both, last):
        both = jnp.concatenate([both, jnp.zeros((2 * HEAD, SPARE), F32)], axis=1)
        if h < HEAD // SPARE:
            moved = pltpu.roll(last, HEAD - SPARE * h, 1) if SPARE * h < HEAD else last
            both = jnp.where(lane_of(both.shape) < HEAD, both, moved)
        first = self.p.c == 0
        rows = row_of(h)
        self.acc[rows, :] = jnp.where(first, both[:HEAD], both[HEAD:])
        self.sc[rows, :] = jnp.where(first, both[HEAD:], both[:HEAD]).astype(BF16)

    def clear(self):
        rows = slice((HEADS - 1) * HEAD, ROWS)
        self.acc[rows, :] = jnp.zeros((PIECE, WIDE), F32)
        self.sc[rows, :] = jnp.zeros((PIECE, WIDE), BF16)

    def pair(self, h):
        if h < HEADS - 1:
            return self.out[0, row_of(h), :], self.out[1, row_of(h), :]
        found = []
        for c in (0, 1):
            whole = jnp.zeros((HEAD, WIDE), F32)
            lane = lane_of(whole.shape)
            for i in range(HEAD // SPARE):
                part = pltpu.roll(self.out[c, row_of(i), :].astype(F32), SPARE * (i + 1), 1)
                here = jnp.logical_and(lane >= SPARE * i, lane < SPARE * (i + 1))
                whole = jnp.where(here, part, whole)
            found.append(whole.astype(BF16))
        return found

    def piece(self, i):
        return pl.ds(pl.multiple_of(i * PIECE, PIECE), PIECE)

    def mine(self):
        return self.piece(self.p.z * FRAMES + self.p.frame)

    def send(self, at, src, dst, peer):
        pltpu.make_async_remote_copy(
            src_ref=src,
            dst_ref=dst,
            send_sem=self.sems.at[2 * at],
            recv_sem=self.sems.at[2 * at + 1],
            device_id=peer,
            device_id_type=MESH,
        ).start()

    def wait(self, sem):
        most = self.sc.at[0 : ROWS - PIECE, :]
        pltpu.make_async_copy(most, most, self.sems.at[sem]).wait()

    def s0(self):
        self.wp = self.l.start(self.sc, self.rc, self.p.core_peer())

    def s1(self):
        self.wp.wait_recv()
        total = self.acc[...] + self.rc[...].astype(F32)
        self.acc[...] = total
        self.sz[...] = total.astype(BF16)
        for e in FAR_FIRST:
            frame, z = self.p.chip(e)
            self.send(0, self.sz.at[self.piece(z * FRAMES + frame), :], self.rz.at[e - 1], self.p.chip_peer(e))

    def s2(self):
        self.wait(1)
        for d in range(FRAMES):
            total = self.acc[self.mine(), :] if d == 0 else self.rz[d - 1].astype(F32)
            for dz in range(1, RING):
                total = total + self.rz[dz * FRAMES + d - 1].astype(F32)
            self.blocks[self.p.behind[d]] = total
        total = jnp.zeros((PIECE, WIDE), F32)
        for f in reversed(range(FRAMES)) if self.reverse else range(FRAMES):
            total = total + self.blocks[f]
            self.sums[f] = total.astype(BF16)
        here = self.out.at[self.p.c, self.mine(), :]
        here[...] = self.sums[self.p.frame]
        for e in FAR_FIRST:
            self.send(1, self.sums.at[self.p.chip(e)[0]], here, self.p.chip_peer(e))

    def s3(self):
        self.wait(3)
        here = self.out.at[self.p.c]
        self.wp = self.l.start(here, here, self.p.core_peer())

    def s4(self):
        self.wp.wait_recv()

    def drain(self):
        self.wait(0)
        self.wait(2)


def small_scratch():
    one = pltpu.VMEM((NROWS, WIDE), F32)
    return [one, pltpu.VMEM((PACK - 1, NROWS, WIDE), F32), one, pltpu.VMEM((FRAMES - 1, NROWS, WIDE), F32), one]


def big_scratch():
    return [
        pltpu.VMEM((ROWS, WIDE), F32),
        pltpu.VMEM((ROWS, WIDE), BF16),
        pltpu.VMEM((ROWS, WIDE), BF16),
        pltpu.VMEM((ROWS, WIDE), BF16),
        pltpu.VMEM((CHIPS - 1, PIECE, WIDE), BF16),
        pltpu.VMEM((FRAMES, PIECE, WIDE), F32),
        pltpu.VMEM((FRAMES, PIECE, WIDE), BF16),
        pltpu.VMEM((2, ROWS, WIDE), BF16),
    ]


COPIES = 2 * (PACK - 1 + FRAMES - 1) + 2 * 2
SPANS = ((1024, 1408), (1408, 2304), (2304, COLS), (0, 256), (256, 1024))


def in_head(rows):
    shape = (rows, HD)
    lane = lax.broadcasted_iota(jnp.int32, shape, 1)
    low = lax.broadcasted_iota(jnp.int32, shape, 0) * HEAD
    return jnp.logical_and(lane >= low, lane < low + HEAD)


def kernel(
    x_hbm, w_hbm, clip_hbm, og_hbm, attv, outv,
    xv, wv, clipv, og, feat, ng, inv, dgs, grads, acc, ncol, dcol,
    lsem, send, recv, ssem, gsem, entry, *rest,
):
    ns, ds_ = rest[:5], rest[5:10]
    bs, bg = rest[10:18], rest[18:26]
    p = Place()
    barrier = pltpu.get_barrier_semaphore()
    peers = p.peers()
    loads = {
        "clip": pltpu.make_async_copy(clip_hbm, clipv, lsem.at[0]),
        "x": pltpu.make_async_copy(x_hbm.at[0], xv, lsem.at[1]),
        "og": pltpu.make_async_copy(og_hbm.at[0], og, lsem.at[2]),
    }
    for i, (lo, hi) in enumerate(SPANS):
        loads[lo] = pltpu.make_async_copy(w_hbm.at[:, lo:hi], wv.at[:, lo:hi], lsem.at[3 + i])
    for name in ("x", 1024, "clip"):
        loads[name].start()
    for peer in peers:
        pl.semaphore_signal(barrier, inc=1, device_id=peer, device_id_type=MESH)

    links = Links(send, recv)
    norm = Small(p, links, ns, False)
    dnorm = Small(p, links, ds_, True)
    state = Big(p, links, bs, ssem, False)
    grad = Big(p, links, bg, gsem, True)

    def project(lo, hi):
        r = tn(wv[:, lo:hi], xv[...])
        pos = min(max(2 * HD - lo, 0), hi - lo)
        if pos:
            feat[lo : lo + pos, :] = jnp.maximum(r[:pos], 0.0).astype(BF16)
        if pos < hi - lo:
            feat[lo + pos : hi, :] = r[pos:].astype(BF16)

    for b in (state, grad):
        b.clear()
    loads["clip"].wait()
    is1 = clipv[...] > 0
    m1 = clipv[...].astype(F32)
    m0 = 1.0 - m1
    m0b, m1b = m0.astype(BF16), m1.astype(BF16)

    def split(v, gap=0):
        parts = [v * m0b, v * m1b]
        if gap:
            zero = jnp.zeros((gap, TOK), BF16)
            parts = [parts[0], zero, parts[1], zero]
        return jnp.concatenate(parts, axis=0)

    def put_rows(ref, r):
        ref[...] = jnp.zeros_like(ref)
        for t in range(TILES):
            width = min(WIDE, HD - t * WIDE)
            ref[2 * t : 2 * t + 2, :width] = r[0:2, t * WIDE : t * WIDE + width]

    def get_rows(ref):
        return jnp.concatenate([ref[2 * t : 2 * t + 2, :] for t in range(TILES)], axis=1)

    def columns(ref, dst):
        for t in range(TILES):
            both = ref[2 * t : 2 * t + 2, :]
            both = jnp.concatenate([both, jnp.zeros((6, WIDE), F32)], axis=0)
            dst[t * WIDE : (t + 1) * WIDE, :] = both.T

    def pick(col, h):
        c = col[row_of(h), :]
        return jnp.where(is1, c[:, 1:2], c[:, 0:1])

    def norm_local():
        side = jnp.concatenate([m0b, m1b, jnp.zeros((14, TOK), BF16)], axis=0)
        put_rows(norm.own, nt(side, feat[HD : 2 * HD, :]))

    def put_all(big, terms):
        last = jnp.concatenate([terms(HEADS - 1), jnp.zeros((2 * HEAD, SPARE), F32)], axis=1)
        for h in range(HEADS - 1):
            big.put(h, terms(h), last)

    def state_local():
        put_all(state, lambda h: nt(split(feat[row_of(HEADS + h), :]), feat[row_of(2 * HEADS + h), :]))

    def denominators():
        rows = get_rows(norm.out)[:, :HD]
        keep = in_head(16)
        side = jnp.concatenate(
            [jnp.where(keep, jnp.broadcast_to(rows[c : c + 1], (16, HD)), 0.0) for c in (0, 1)], axis=0
        )
        den = nn(side.astype(BF16), feat[:HD, :])
        inv[...] = 1.0 / (jnp.where(is1, den[16:], den[:16]) + EPS)
        columns(norm.out, ncol)

    def grad_local():
        def terms(h):
            v = (og[row_of(h), :].astype(F32) * inv[h : h + 1, :]).astype(BF16)
            ng[row_of(h), :] = v
            return nt(split(feat[row_of(h), :]), v)

        put_all(grad, terms)

    def attend():
        for h in range(HEADS):
            q = feat[row_of(h), :]
            s0, s1 = state.pair(h)
            r = inv[h : h + 1, :]
            att = tn(jnp.concatenate([s0, s1], axis=0), split(q))[:HEAD] * r
            attv[0, row_of(h), :] = att.astype(BF16)
            d = -jnp.sum(og[row_of(h), :].astype(F32) * att, axis=0, keepdims=True) * r
            dgs[h : h + 1, :] = d
            qg = nn(jnp.concatenate([s0, s1], axis=1), split(ng[row_of(h), :], WIDE - HEAD))
            qg = qg + d * pick(ncol, h)
            grads[row_of(h), :] = jnp.where(q.astype(F32) > 0, qg, 0.0).astype(BF16)

    def dnorm_local():
        d = dgs[...]
        both = jnp.concatenate([d * m0, d * m1], axis=0)
        hi = both.astype(BF16)
        lo = (both - hi.astype(F32)).astype(BF16)
        r = nt(jnp.concatenate([hi, lo], axis=0), feat[:HD, :])
        r = r[:32] + r[32:]
        keep = in_head(16)
        rows = [
            jnp.sum(jnp.where(keep, r[16 * c : 16 * c + 16], 0.0), axis=0, keepdims=True) for c in (0, 1)
        ]
        put_rows(dnorm.own, jnp.concatenate(rows, axis=0))

    def value_grads():
        for h in range(HEADS):
            g0, g1 = grad.pair(h)
            r = tn(jnp.concatenate([g0, g1], axis=0), split(feat[row_of(HEADS + h), :]))
            grads[row_of(2 * HEADS + h), :] = r[:HEAD].astype(BF16)

    def key_grads():
        for h in range(HEADS):
            g0, g1 = grad.pair(h)
            v = feat[row_of(2 * HEADS + h), :]
            kg = nn(jnp.concatenate([g0, g1], axis=1), split(v, WIDE - HEAD)) + pick(dcol, h)
            keep = feat[row_of(HEADS + h), :].astype(F32) > 0
            grads[row_of(HEADS + h), :] = jnp.where(keep, kg, 0.0).astype(BF16)

    def back(lo, hi, kind):
        for m in (0, 1):
            rows = slice(m * HD, (m + 1) * HD)
            r = nn(wv[rows, lo:hi], grads[lo:hi, :])
            if kind > 0:
                r = r + acc[rows, :]
            if kind < 2:
                acc[rows, :] = r
            else:
                outv[0, rows, :] = r.astype(BF16)

    loads["x"].wait()
    loads[1024].wait()
    loads[1408].start()
    loads[2304].start()
    project(1024, 1408)
    loads[1408].wait()
    loads[0].start()
    loads[256].start()
    project(1408, 2304)
    norm_local()
    pl.semaphore_wait(barrier, len(peers))
    norm.s0()
    for peer in p.frame_peers():
        pl.semaphore_signal(entry, inc=1, device_id=peer, device_id_type=MESH)
    loads[2304].wait()
    loads["og"].start()
    project(2304, COLS)
    state_local()
    state.s0()
    norm.s1()
    loads[0].wait()
    project(0, 256)
    pl.semaphore_wait(entry, FRAMES - 1)
    state.s1()
    loads[256].wait()
    project(256, 1024)
    loads["og"].wait()
    norm.s2()
    denominators()
    grad_local()
    grad.s0()
    grad.s1()
    state.s2()
    grad.s2()
    state.s3()
    state.s4()
    attend()
    dnorm_local()
    dnorm.s0()
    back(0, 1024, 0)
    grad.s3()
    dnorm.s1()
    grad.s4()
    value_grads()
    back(2304, COLS, 1)
    dnorm.s2()
    columns(dnorm.out, dcol)
    key_grads()
    back(1024, 2304, 2)
    state.drain()
    grad.drain()
    links.drain()


def per_device(inputs, weight, clip_of_row, out_grad):
    anywhere = pl.BlockSpec(memory_space=pl.ANY)
    att, grad = pl.pallas_call(
        kernel,
        out_shape=(pltpu.VMEM((1, HD, TOK), BF16), pltpu.VMEM((1, D, TOK), BF16)),
        in_specs=[anywhere] * 4,
        out_specs=(pl.BlockSpec(memory_space=pltpu.VMEM),) * 2,
        scratch_shapes=[
            pltpu.VMEM((D, TOK), BF16),
            pltpu.VMEM((D, COLS), BF16),
            pltpu.VMEM((1, TOK), jnp.int32),
            pltpu.VMEM((HD, TOK), BF16),
            pltpu.VMEM((COLS, TOK), BF16),
            pltpu.VMEM((HD, TOK), BF16),
            pltpu.VMEM((16, TOK), F32),
            pltpu.VMEM((16, TOK), F32),
            pltpu.VMEM((COLS, TOK), BF16),
            pltpu.VMEM((D, TOK), F32),
            pltpu.VMEM((TILES * WIDE, 8), F32),
            pltpu.VMEM((TILES * WIDE, 8), F32),
            pltpu.SemaphoreType.DMA((8,)),
            pltpu.SemaphoreType.DMA((COPIES,)),
            pltpu.SemaphoreType.DMA((COPIES,)),
            pltpu.SemaphoreType.DMA((4,)),
            pltpu.SemaphoreType.DMA((4,)),
            pltpu.SemaphoreType.REGULAR,
            *small_scratch(),
            *small_scratch(),
            *big_scratch(),
            *big_scratch(),
        ],
        compiler_params=pltpu.CompilerParams(
            collective_id=0, has_side_effects=True, vmem_limit_bytes=54000000
        ),
    )(inputs.swapaxes(1, 2), weight, clip_of_row, out_grad.swapaxes(1, 2))
    return att.swapaxes(1, 2), grad.swapaxes(1, 2)


def solution(mesh):
    placed = (P("frame", "pack", None), P(), P("frame", "pack"), P("frame", "pack", None))
    return jax.shard_map(
        per_device,
        mesh=mesh,
        in_specs=placed,
        out_specs=(P("frame", "pack", None), P("frame", "pack", None)),
        check_vma=False,
    )
```

```python
import jax
import jax.numpy as jnp
from jax import lax
from jax.experimental import pallas as pl
from jax.experimental.pallas import tpu as pltpu
from jax.sharding import PartitionSpec as P

F32 = jnp.float32
BF16 = jnp.bfloat16
MESH = pl.DeviceIdType.MESH
EPS = 1e-06
HEAD = 112
HEADS = 10
WIDE = 128
TOK = 512
D = 2240
HD = HEADS * HEAD
COLS = 3 * HD
RING = 4
PACK = 2 * RING
FRAMES = RING * RING
CHIPS = RING * FRAMES
PIECE = 16
ROWS = CHIPS * PIECE
SPARE = WIDE - HEAD
NROWS = 24
TILES = 9


def tn(a, b):
    return lax.dot_general(a, b, (((0,), (0,)), ((), ())), preferred_element_type=F32)


def nt(a, b):
    return lax.dot_general(a, b, (((1,), (1,)), ((), ())), preferred_element_type=F32)


def nn(a, b):
    return lax.dot_general(a, b, (((1,), (0,)), ((), ())), preferred_element_type=F32)


def row_of(h):
    return slice(h * HEAD, (h + 1) * HEAD)


def hops(e):
    return sum(min(d, RING - d) for d in (e // FRAMES, (e % FRAMES) // RING, e % RING))


FAR_FIRST = sorted(range(1, CHIPS), key=lambda e: (-hops(e), e))


class Place:
    def __init__(self):
        self.frame = lax.axis_index("frame")
        self.pack = lax.axis_index("pack")
        x, y = lax.div(self.frame, RING), lax.rem(self.frame, RING)
        z, c = lax.div(self.pack, 2), lax.rem(self.pack, 2)
        self.z, self.c = z, c
        self.cs = [c, 1 - c]
        self.zs = [z] + [lax.rem(z + d, RING) for d in range(1, RING)]
        self.ahead = self.grid(x, y, 1)
        self.behind = self.grid(x, y, RING - 1)

    def grid(self, x, y, step):
        xs = [lax.rem(x + step * d, RING) * RING for d in range(RING)]
        ys = [lax.rem(y + step * d, RING) for d in range(RING)]
        return [u + v for u in xs for v in ys]

    def core_peer(self):
        return self.pack_peer(0)

    def chip(self, e):
        return self.ahead[e % FRAMES], self.zs[e // FRAMES]

    def chip_peer(self, e):
        frame, z = self.chip(e)
        return {"frame": frame, "pack": z * 2 + self.c}

    def pack_peer(self, k):
        dz, flip = divmod(k + 1, 2)
        return {"frame": self.frame, "pack": self.zs[dz] * 2 + self.cs[flip]}

    def frame_peer(self, j):
        return {"frame": lax.rem(self.frame + (j % FRAMES), FRAMES), "pack": self.pack}

    def peers(self):
        return [self.pack_peer(k) for k in range(PACK - 1)] + self.frame_peers()

    def frame_peers(self):
        return [self.frame_peer(j) for j in range(1, FRAMES)]


class Links:
    def __init__(self, send, recv):
        self.send, self.recv, self.at, self.copies = send, recv, 0, []

    def start(self, src, dst, device, when=None):
        copy = pltpu.make_async_remote_copy(
            src_ref=src,
            dst_ref=dst,
            send_sem=self.send.at[self.at],
            recv_sem=self.recv.at[self.at],
            device_id=device,
            device_id_type=MESH,
        )
        self.at += 1
        if when is None:
            copy.start()
        else:
            pl.when(when)(copy.start)
        self.copies.append((copy, when))
        return copy

    def drain(self):
        for copy, when in self.copies:
            if when is None:
                copy.wait_send()
            else:
                pl.when(when)(copy.wait_send)


class Frames:
    def __init__(self, place, links, reverse):
        self.p, self.l, self.reverse = place, links, reverse

    def spread(self, src, slots):
        f = self.p.frame
        self.w = []
        for j in sorted(range(1, FRAMES), key=lambda j: (-hops(j), j)):
            to, into = (f >= j, f + j < FRAMES) if self.reverse else (f + j < FRAMES, f >= j)
            peer = self.p.frame_peer(-j if self.reverse else j)
            self.w.append((self.l.start(src, slots.at[j - 1], peer, to), into, j - 1))

    def total(self, own, slots):
        for copy, into, _ in self.w:
            pl.when(into)(copy.wait_recv)
        for _, into, slot in self.w:
            own = own + jnp.where(into, slots[slot], 0.0)
        return own


class Small(Frames):
    def __init__(self, place, links, refs, reverse):
        super().__init__(place, links, reverse)
        self.own, self.rz, self.sy, self.ry, self.out = refs

    def s0(self):
        self.wp = [
            self.l.start(self.own, self.rz.at[k], self.p.pack_peer(k)) for k in range(PACK - 1)
        ]

    def s1(self):
        for w in self.wp:
            w.wait_recv()
        total = self.own[...]
        for k in range(PACK - 1):
            total = total + self.rz[k]
        self.sy[...] = total
        self.spread(self.sy, self.ry)

    def s2(self):
        self.out[...] = self.total(self.sy[...], self.ry).astype(BF16).astype(F32)


def lane_of(shape):
    return lax.broadcasted_iota(jnp.int32, shape, 1)


class Big:
    def __init__(self, place, links, refs, sems, reverse):
        self.p, self.l, self.reverse, self.sems = place, links, reverse, sems
        self.acc, self.sc, self.rc, self.sz, self.rz, self.blocks, self.sums, self.out = refs

    def put(self, h, both, last):
        both = jnp.concatenate([both, jnp.zeros((2 * HEAD, SPARE), F32)], axis=1)
        if h < HEAD // SPARE:
            moved = pltpu.roll(last, HEAD - SPARE * h, 1) if SPARE * h < HEAD else last
            both = jnp.where(lane_of(both.shape) < HEAD, both, moved)
        first = self.p.c == 0
        rows = row_of(h)
        self.acc[rows, :] = jnp.where(first, both[:HEAD], both[HEAD:])
        self.sc[rows, :] = jnp.where(first, both[HEAD:], both[:HEAD]).astype(BF16)

    def clear(self):
        rows = slice((HEADS - 1) * HEAD, ROWS)
        self.acc[rows, :] = jnp.zeros((PIECE, WIDE), F32)
        self.sc[rows, :] = jnp.zeros((PIECE, WIDE), BF16)

    def pair(self, h):
        if h < HEADS - 1:
            return self.out[0, row_of(h), :], self.out[1, row_of(h), :]
        found = []
        for c in (0, 1):
            whole = jnp.zeros((HEAD, WIDE), F32)
            lane = lane_of(whole.shape)
            for i in range(HEAD // SPARE):
                part = pltpu.roll(self.out[c, row_of(i), :].astype(F32), SPARE * (i + 1), 1)
                here = jnp.logical_and(lane >= SPARE * i, lane < SPARE * (i + 1))
                whole = jnp.where(here, part, whole)
            found.append(whole.astype(BF16))
        return found

    def piece(self, i):
        return pl.ds(pl.multiple_of(i * PIECE, PIECE), PIECE)

    def mine(self):
        return self.piece(self.p.z * FRAMES + self.p.frame)

    def send(self, at, src, dst, peer):
        pltpu.make_async_remote_copy(
            src_ref=src,
            dst_ref=dst,
            send_sem=self.sems.at[2 * at],
            recv_sem=self.sems.at[2 * at + 1],
            device_id=peer,
            device_id_type=MESH,
        ).start()

    def wait(self, sem):
        most = self.sc.at[0 : ROWS - PIECE, :]
        pltpu.make_async_copy(most, most, self.sems.at[sem]).wait()

    def s0(self):
        self.wp = self.l.start(self.sc, self.rc, self.p.core_peer())

    def s1(self):
        self.wp.wait_recv()
        total = self.acc[...] + self.rc[...].astype(F32)
        self.acc[...] = total
        self.sz[...] = total.astype(BF16)
        for e in FAR_FIRST:
            frame, z = self.p.chip(e)
            self.send(0, self.sz.at[self.piece(z * FRAMES + frame), :], self.rz.at[e - 1], self.p.chip_peer(e))

    def s2(self):
        self.wait(1)
        for d in range(FRAMES):
            total = self.acc[self.mine(), :] if d == 0 else self.rz[d - 1].astype(F32)
            for dz in range(1, RING):
                total = total + self.rz[dz * FRAMES + d - 1].astype(F32)
            self.blocks[self.p.behind[d]] = total
        total = jnp.zeros((PIECE, WIDE), F32)
        for f in reversed(range(FRAMES)) if self.reverse else range(FRAMES):
            total = total + self.blocks[f]
            self.sums[f] = total.astype(BF16)
        here = self.out.at[self.p.c, self.mine(), :]
        here[...] = self.sums[self.p.frame]
        for e in FAR_FIRST:
            self.send(1, self.sums.at[self.p.chip(e)[0]], here, self.p.chip_peer(e))

    def s3(self):
        self.wait(3)
        here = self.out.at[self.p.c]
        self.wp = self.l.start(here, here, self.p.core_peer())

    def s4(self):
        self.wp.wait_recv()

    def drain(self):
        self.wait(0)
        self.wait(2)


def small_scratch():
    one = pltpu.VMEM((NROWS, WIDE), F32)
    return [one, pltpu.VMEM((PACK - 1, NROWS, WIDE), F32), one, pltpu.VMEM((FRAMES - 1, NROWS, WIDE), F32), one]


def big_scratch():
    return [
        pltpu.VMEM((ROWS, WIDE), F32),
        pltpu.VMEM((ROWS, WIDE), BF16),
        pltpu.VMEM((ROWS, WIDE), BF16),
        pltpu.VMEM((ROWS, WIDE), BF16),
        pltpu.VMEM((CHIPS - 1, PIECE, WIDE), BF16),
        pltpu.VMEM((FRAMES, PIECE, WIDE), F32),
        pltpu.VMEM((FRAMES, PIECE, WIDE), BF16),
        pltpu.VMEM((2, ROWS, WIDE), BF16),
    ]


COPIES = 2 * (PACK - 1 + FRAMES - 1) + 2 * 2
SPANS = ((1024, 1408), (1408, 2304), (2304, COLS), (0, 256), (256, 1024))


def in_head(rows):
    shape = (rows, HD)
    lane = lax.broadcasted_iota(jnp.int32, shape, 1)
    low = lax.broadcasted_iota(jnp.int32, shape, 0) * HEAD
    return jnp.logical_and(lane >= low, lane < low + HEAD)


def kernel(
    x_hbm, w_hbm, clip_hbm, og_hbm, attv, outv,
    xv, wv, clipv, og, feat, ng, inv, dgs, grads, acc, ncol, dcol,
    lsem, send, recv, ssem, gsem, entry, *rest,
):
    ns, ds_ = rest[:5], rest[5:10]
    bs, bg = rest[10:18], rest[18:26]
    p = Place()
    barrier = pltpu.get_barrier_semaphore()
    peers = p.peers()
    loads = {
        "clip": pltpu.make_async_copy(clip_hbm, clipv, lsem.at[0]),
        "x": pltpu.make_async_copy(x_hbm.at[0], xv, lsem.at[1]),
        "og": pltpu.make_async_copy(og_hbm.at[0], og, lsem.at[2]),
    }
    for i, (lo, hi) in enumerate(SPANS):
        loads[lo] = pltpu.make_async_copy(w_hbm.at[:, lo:hi], wv.at[:, lo:hi], lsem.at[3 + i])
    for name in ("x", 1024, "clip"):
        loads[name].start()
    for peer in peers:
        pl.semaphore_signal(barrier, inc=1, device_id=peer, device_id_type=MESH)

    links = Links(send, recv)
    norm = Small(p, links, ns, False)
    dnorm = Small(p, links, ds_, True)
    state = Big(p, links, bs, ssem, False)
    grad = Big(p, links, bg, gsem, True)

    def project(lo, hi):
        r = tn(wv[:, lo:hi], xv[...])
        pos = min(max(2 * HD - lo, 0), hi - lo)
        if pos:
            feat[lo : lo + pos, :] = jnp.maximum(r[:pos], 0.0).astype(BF16)
        if pos < hi - lo:
            feat[lo + pos : hi, :] = r[pos:].astype(BF16)

    for b in (state, grad):
        b.clear()
    loads["clip"].wait()
    is1 = clipv[...] > 0
    m1 = clipv[...].astype(F32)
    m0 = 1.0 - m1
    m0b, m1b = m0.astype(BF16), m1.astype(BF16)

    def split(v, gap=0):
        parts = [v * m0b, v * m1b]
        if gap:
            zero = jnp.zeros((gap, TOK), BF16)
            parts = [parts[0], zero, parts[1], zero]
        return jnp.concatenate(parts, axis=0)

    def put_rows(ref, r):
        ref[...] = jnp.zeros_like(ref)
        for t in range(TILES):
            width = min(WIDE, HD - t * WIDE)
            ref[2 * t : 2 * t + 2, :width] = r[0:2, t * WIDE : t * WIDE + width]

    def get_rows(ref):
        return jnp.concatenate([ref[2 * t : 2 * t + 2, :] for t in range(TILES)], axis=1)

    def columns(ref, dst):
        for t in range(TILES):
            both = ref[2 * t : 2 * t + 2, :]
            both = jnp.concatenate([both, jnp.zeros((6, WIDE), F32)], axis=0)
            dst[t * WIDE : (t + 1) * WIDE, :] = both.T

    def pick(col, h):
        c = col[row_of(h), :]
        return jnp.where(is1, c[:, 1:2], c[:, 0:1])

    def norm_local():
        side = jnp.concatenate([m0b, m1b, jnp.zeros((14, TOK), BF16)], axis=0)
        put_rows(norm.own, nt(side, feat[HD : 2 * HD, :]))

    def put_all(big, terms):
        last = jnp.concatenate([terms(HEADS - 1), jnp.zeros((2 * HEAD, SPARE), F32)], axis=1)
        for h in range(HEADS - 1):
            big.put(h, terms(h), last)

    def state_local():
        put_all(state, lambda h: nt(split(feat[row_of(HEADS + h), :]), feat[row_of(2 * HEADS + h), :]))

    def denominators():
        rows = get_rows(norm.out)[:, :HD]
        keep = in_head(16)
        side = jnp.concatenate(
            [jnp.where(keep, jnp.broadcast_to(rows[c : c + 1], (16, HD)), 0.0) for c in (0, 1)], axis=0
        )
        den = nn(side.astype(BF16), feat[:HD, :])
        inv[...] = 1.0 / (jnp.where(is1, den[16:], den[:16]) + EPS)
        columns(norm.out, ncol)

    def grad_local():
        def terms(h):
            v = (og[row_of(h), :].astype(F32) * inv[h : h + 1, :]).astype(BF16)
            ng[row_of(h), :] = v
            return nt(split(feat[row_of(h), :]), v)

        put_all(grad, terms)

    def attend():
        for h in range(HEADS):
            q = feat[row_of(h), :]
            s0, s1 = state.pair(h)
            r = inv[h : h + 1, :]
            att = tn(jnp.concatenate([s0, s1], axis=0), split(q))[:HEAD] * r
            attv[0, row_of(h), :] = att.astype(BF16)
            d = -jnp.sum(og[row_of(h), :].astype(F32) * att, axis=0, keepdims=True) * r
            dgs[h : h + 1, :] = d
            qg = nn(jnp.concatenate([s0, s1], axis=1), split(ng[row_of(h), :], WIDE - HEAD))
            qg = qg + d * pick(ncol, h)
            grads[row_of(h), :] = jnp.where(q.astype(F32) > 0, qg, 0.0).astype(BF16)

    def dnorm_local():
        d = dgs[...]
        both = jnp.concatenate([d * m0, d * m1], axis=0)
        hi = both.astype(BF16)
        lo = (both - hi.astype(F32)).astype(BF16)
        r = nt(jnp.concatenate([hi, lo], axis=0), feat[:HD, :])
        r = r[:32] + r[32:]
        keep = in_head(16)
        rows = [
            jnp.sum(jnp.where(keep, r[16 * c : 16 * c + 16], 0.0), axis=0, keepdims=True) for c in (0, 1)
        ]
        put_rows(dnorm.own, jnp.concatenate(rows, axis=0))

    def value_grads():
        for h in range(HEADS):
            g0, g1 = grad.pair(h)
            r = tn(jnp.concatenate([g0, g1], axis=0), split(feat[row_of(HEADS + h), :]))
            grads[row_of(2 * HEADS + h), :] = r[:HEAD].astype(BF16)

    def key_grads():
        for h in range(HEADS):
            g0, g1 = grad.pair(h)
            v = feat[row_of(2 * HEADS + h), :]
            kg = nn(jnp.concatenate([g0, g1], axis=1), split(v, WIDE - HEAD)) + pick(dcol, h)
            keep = feat[row_of(HEADS + h), :].astype(F32) > 0
            grads[row_of(HEADS + h), :] = jnp.where(keep, kg, 0.0).astype(BF16)

    def back(lo, hi, kind):
        for m in (0, 1):
            rows = slice(m * HD, (m + 1) * HD)
            r = nn(wv[rows, lo:hi], grads[lo:hi, :])
            if kind > 0:
                r = r + acc[rows, :]
            if kind < 2:
                acc[rows, :] = r
            else:
                outv[0, rows, :] = r.astype(BF16)

    loads["x"].wait()
    loads[1024].wait()
    loads[1408].start()
    loads[2304].start()
    project(1024, 1408)
    loads[1408].wait()
    loads[0].start()
    loads[256].start()
    project(1408, 2304)
    norm_local()
    pl.semaphore_wait(barrier, len(peers))
    norm.s0()
    for peer in p.frame_peers():
        pl.semaphore_signal(entry, inc=1, device_id=peer, device_id_type=MESH)
    loads[2304].wait()
    loads["og"].start()
    project(2304, COLS)
    norm.s1()
    state_local()
    state.s0()
    loads[0].wait()
    project(0, 256)
    pl.semaphore_wait(entry, FRAMES - 1)
    state.s1()
    loads[256].wait()
    project(256, 1024)
    loads["og"].wait()
    norm.s2()
    denominators()
    grad_local()
    grad.s0()
    grad.s1()
    state.s2()
    grad.s2()
    state.s3()
    state.s4()
    attend()
    dnorm_local()
    dnorm.s0()
    back(0, 1024, 0)
    dnorm.s1()
    grad.s3()
    grad.s4()
    value_grads()
    back(2304, COLS, 1)
    dnorm.s2()
    columns(dnorm.out, dcol)
    key_grads()
    back(1024, 2304, 2)
    state.drain()
    grad.drain()
    links.drain()


def per_device(inputs, weight, clip_of_row, out_grad):
    anywhere = pl.BlockSpec(memory_space=pl.ANY)
    att, grad = pl.pallas_call(
        kernel,
        out_shape=(pltpu.VMEM((1, HD, TOK), BF16), pltpu.VMEM((1, D, TOK), BF16)),
        in_specs=[anywhere] * 4,
        out_specs=(pl.BlockSpec(memory_space=pltpu.VMEM),) * 2,
        scratch_shapes=[
            pltpu.VMEM((D, TOK), BF16),
            pltpu.VMEM((D, COLS), BF16),
            pltpu.VMEM((1, TOK), jnp.int32),
            pltpu.VMEM((HD, TOK), BF16),
            pltpu.VMEM((COLS, TOK), BF16),
            pltpu.VMEM((HD, TOK), BF16),
            pltpu.VMEM((16, TOK), F32),
            pltpu.VMEM((16, TOK), F32),
            pltpu.VMEM((COLS, TOK), BF16),
            pltpu.VMEM((D, TOK), F32),
            pltpu.VMEM((TILES * WIDE, 8), F32),
            pltpu.VMEM((TILES * WIDE, 8), F32),
            pltpu.SemaphoreType.DMA((8,)),
            pltpu.SemaphoreType.DMA((COPIES,)),
            pltpu.SemaphoreType.DMA((COPIES,)),
            pltpu.SemaphoreType.DMA((4,)),
            pltpu.SemaphoreType.DMA((4,)),
            pltpu.SemaphoreType.REGULAR,
            *small_scratch(),
            *small_scratch(),
            *big_scratch(),
            *big_scratch(),
        ],
        compiler_params=pltpu.CompilerParams(
            collective_id=0, has_side_effects=True, vmem_limit_bytes=54000000
        ),
    )(inputs.swapaxes(1, 2), weight, clip_of_row, out_grad.swapaxes(1, 2))
    return att.swapaxes(1, 2), grad.swapaxes(1, 2)


def solution(mesh):
    placed = (P("frame", "pack", None), P(), P("frame", "pack"), P("frame", "pack", None))
    return jax.shard_map(
        per_device,
        mesh=mesh,
        in_specs=placed,
        out_specs=(P("frame", "pack", None), P("frame", "pack", None)),
        check_vma=False,
    )
```

```python
import jax
import jax.numpy as jnp
from jax import lax
from jax.experimental import pallas as pl
from jax.experimental.pallas import tpu as pltpu
from jax.sharding import PartitionSpec as P

F32 = jnp.float32
BF16 = jnp.bfloat16
MESH = pl.DeviceIdType.MESH
EPS = 1e-06
HEAD = 112
HEADS = 10
WIDE = 128
TOK = 512
D = 2240
HD = HEADS * HEAD
COLS = 3 * HD
RING = 4
PACK = 2 * RING
FRAMES = RING * RING
CHIPS = RING * FRAMES
PIECE = 16
ROWS = CHIPS * PIECE
SPARE = WIDE - HEAD
NROWS = 24
TILES = 9


def tn(a, b):
    return lax.dot_general(a, b, (((0,), (0,)), ((), ())), preferred_element_type=F32)


def nt(a, b):
    return lax.dot_general(a, b, (((1,), (1,)), ((), ())), preferred_element_type=F32)


def nn(a, b):
    return lax.dot_general(a, b, (((1,), (0,)), ((), ())), preferred_element_type=F32)


def row_of(h):
    return slice(h * HEAD, (h + 1) * HEAD)


def hops(e):
    return sum(min(d, RING - d) for d in (e // FRAMES, (e % FRAMES) // RING, e % RING))


FAR_FIRST = sorted(range(1, CHIPS), key=lambda e: (-hops(e), e))


class Place:
    def __init__(self):
        self.frame = lax.axis_index("frame")
        self.pack = lax.axis_index("pack")
        x, y = lax.div(self.frame, RING), lax.rem(self.frame, RING)
        z, c = lax.div(self.pack, 2), lax.rem(self.pack, 2)
        self.z, self.c = z, c
        self.cs = [c, 1 - c]
        self.zs = [z] + [lax.rem(z + d, RING) for d in range(1, RING)]
        self.ahead = self.grid(x, y, 1)
        self.behind = self.grid(x, y, RING - 1)

    def grid(self, x, y, step):
        xs = [lax.rem(x + step * d, RING) * RING for d in range(RING)]
        ys = [lax.rem(y + step * d, RING) for d in range(RING)]
        return [u + v for u in xs for v in ys]

    def core_peer(self):
        return self.pack_peer(0)

    def chip(self, e):
        return self.ahead[e % FRAMES], self.zs[e // FRAMES]

    def chip_peer(self, e):
        frame, z = self.chip(e)
        return {"frame": frame, "pack": z * 2 + self.c}

    def pack_peer(self, k):
        dz, flip = divmod(k + 1, 2)
        return {"frame": self.frame, "pack": self.zs[dz] * 2 + self.cs[flip]}

    def frame_peer(self, j):
        return {"frame": lax.rem(self.frame + (j % FRAMES), FRAMES), "pack": self.pack}

    def peers(self):
        return [self.pack_peer(k) for k in range(PACK - 1)] + self.frame_peers()

    def frame_peers(self):
        return [self.frame_peer(j) for j in range(1, FRAMES)]


class Links:
    def __init__(self, send, recv):
        self.send, self.recv, self.at, self.copies = send, recv, 0, []

    def start(self, src, dst, device, when=None):
        copy = pltpu.make_async_remote_copy(
            src_ref=src,
            dst_ref=dst,
            send_sem=self.send.at[self.at],
            recv_sem=self.recv.at[self.at],
            device_id=device,
            device_id_type=MESH,
        )
        self.at += 1
        if when is None:
            copy.start()
        else:
            pl.when(when)(copy.start)
        self.copies.append((copy, when))
        return copy

    def drain(self):
        for copy, when in self.copies:
            if when is None:
                copy.wait_send()
            else:
                pl.when(when)(copy.wait_send)


class Frames:
    def __init__(self, place, links, reverse):
        self.p, self.l, self.reverse = place, links, reverse

    def spread(self, src, slots):
        f = self.p.frame
        self.w = []
        for j in sorted(range(1, FRAMES), key=lambda j: (-hops(j), j)):
            to, into = (f >= j, f + j < FRAMES) if self.reverse else (f + j < FRAMES, f >= j)
            peer = self.p.frame_peer(-j if self.reverse else j)
            self.w.append((self.l.start(src, slots.at[j - 1], peer, to), into, j - 1))

    def total(self, own, slots):
        for copy, into, _ in self.w:
            pl.when(into)(copy.wait_recv)
        for _, into, slot in self.w:
            own = own + jnp.where(into, slots[slot], 0.0)
        return own


class Small(Frames):
    def __init__(self, place, links, refs, reverse):
        super().__init__(place, links, reverse)
        self.own, self.rz, self.sy, self.ry, self.out = refs

    def s0(self):
        self.wp = [
            self.l.start(self.own, self.rz.at[k], self.p.pack_peer(k)) for k in range(PACK - 1)
        ]

    def s1(self):
        for w in self.wp:
            w.wait_recv()
        total = self.own[...]
        for k in range(PACK - 1):
            total = total + self.rz[k]
        self.sy[...] = total
        self.spread(self.sy, self.ry)

    def s2(self):
        self.out[...] = self.total(self.sy[...], self.ry).astype(BF16).astype(F32)


def lane_of(shape):
    return lax.broadcasted_iota(jnp.int32, shape, 1)


class Big:
    def __init__(self, place, links, refs, sems, reverse):
        self.p, self.l, self.reverse, self.sems = place, links, reverse, sems
        self.acc, self.sc, self.rc, self.sz, self.rz, self.blocks, self.sums, self.out = refs

    def put(self, h, both, last):
        both = jnp.concatenate([both, jnp.zeros((2 * HEAD, SPARE), F32)], axis=1)
        if h < HEAD // SPARE:
            moved = pltpu.roll(last, HEAD - SPARE * h, 1) if SPARE * h < HEAD else last
            both = jnp.where(lane_of(both.shape) < HEAD, both, moved)
        first = self.p.c == 0
        rows = row_of(h)
        self.acc[rows, :] = jnp.where(first, both[:HEAD], both[HEAD:])
        self.sc[rows, :] = jnp.where(first, both[HEAD:], both[:HEAD]).astype(BF16)

    def clear(self):
        rows = slice((HEADS - 1) * HEAD, ROWS)
        self.acc[rows, :] = jnp.zeros((PIECE, WIDE), F32)
        self.sc[rows, :] = jnp.zeros((PIECE, WIDE), BF16)

    def pair(self, h):
        if h < HEADS - 1:
            return self.out[0, row_of(h), :], self.out[1, row_of(h), :]
        found = []
        for c in (0, 1):
            whole = jnp.zeros((HEAD, WIDE), F32)
            lane = lane_of(whole.shape)
            for i in range(HEAD // SPARE):
                part = pltpu.roll(self.out[c, row_of(i), :].astype(F32), SPARE * (i + 1), 1)
                here = jnp.logical_and(lane >= SPARE * i, lane < SPARE * (i + 1))
                whole = jnp.where(here, part, whole)
            found.append(whole.astype(BF16))
        return found

    def piece(self, i):
        return pl.ds(pl.multiple_of(i * PIECE, PIECE), PIECE)

    def mine(self):
        return self.piece(self.p.z * FRAMES + self.p.frame)

    def send(self, at, src, dst, peer):
        pltpu.make_async_remote_copy(
            src_ref=src,
            dst_ref=dst,
            send_sem=self.sems.at[2 * at],
            recv_sem=self.sems.at[2 * at + 1],
            device_id=peer,
            device_id_type=MESH,
        ).start()

    def wait(self, sem):
        most = self.sc.at[0 : ROWS - PIECE, :]
        pltpu.make_async_copy(most, most, self.sems.at[sem]).wait()

    def s0(self):
        self.wp = self.l.start(self.sc, self.rc, self.p.core_peer())

    def s1(self):
        self.wp.wait_recv()
        total = self.acc[...] + self.rc[...].astype(F32)
        self.acc[...] = total
        self.sz[...] = total.astype(BF16)
        for e in FAR_FIRST:
            frame, z = self.p.chip(e)
            self.send(0, self.sz.at[self.piece(z * FRAMES + frame), :], self.rz.at[e - 1], self.p.chip_peer(e))

    def s2(self):
        self.wait(1)
        for d in range(FRAMES):
            total = self.acc[self.mine(), :] if d == 0 else self.rz[d - 1].astype(F32)
            for dz in range(1, RING):
                total = total + self.rz[dz * FRAMES + d - 1].astype(F32)
            self.blocks[self.p.behind[d]] = total
        total = jnp.zeros((PIECE, WIDE), F32)
        for f in reversed(range(FRAMES)) if self.reverse else range(FRAMES):
            total = total + self.blocks[f]
            self.sums[f] = total.astype(BF16)
        here = self.out.at[self.p.c, self.mine(), :]
        here[...] = self.sums[self.p.frame]
        for e in FAR_FIRST:
            self.send(1, self.sums.at[self.p.chip(e)[0]], here, self.p.chip_peer(e))

    def s3(self):
        self.wait(3)
        here = self.out.at[self.p.c]
        self.wp = self.l.start(here, here, self.p.core_peer())

    def s4(self):
        self.wp.wait_recv()

    def drain(self):
        self.wait(0)
        self.wait(2)


def small_scratch():
    one = pltpu.VMEM((NROWS, WIDE), F32)
    return [one, pltpu.VMEM((PACK - 1, NROWS, WIDE), F32), one, pltpu.VMEM((FRAMES - 1, NROWS, WIDE), F32), one]


def big_scratch():
    return [
        pltpu.VMEM((ROWS, WIDE), F32),
        pltpu.VMEM((ROWS, WIDE), BF16),
        pltpu.VMEM((ROWS, WIDE), BF16),
        pltpu.VMEM((ROWS, WIDE), BF16),
        pltpu.VMEM((CHIPS - 1, PIECE, WIDE), BF16),
        pltpu.VMEM((FRAMES, PIECE, WIDE), F32),
        pltpu.VMEM((FRAMES, PIECE, WIDE), BF16),
        pltpu.VMEM((2, ROWS, WIDE), BF16),
    ]


COPIES = 2 * (PACK - 1 + FRAMES - 1) + 2 * 2
SPANS = ((1024, 1408), (1408, 2304), (2304, COLS), (0, 256), (256, 1024))


def in_head(rows):
    shape = (rows, HD)
    lane = lax.broadcasted_iota(jnp.int32, shape, 1)
    low = lax.broadcasted_iota(jnp.int32, shape, 0) * HEAD
    return jnp.logical_and(lane >= low, lane < low + HEAD)


def kernel(
    x_hbm, w_hbm, clip_hbm, og_hbm, attv, outv,
    xv, wv, clipv, og, feat, ng, inv, dgs, grads, acc, ncol, dcol,
    lsem, send, recv, ssem, gsem, entry, *rest,
):
    ns, ds_ = rest[:5], rest[5:10]
    bs, bg = rest[10:18], rest[18:26]
    p = Place()
    barrier = pltpu.get_barrier_semaphore()
    peers = p.peers()
    loads = {
        "clip": pltpu.make_async_copy(clip_hbm, clipv, lsem.at[0]),
        "x": pltpu.make_async_copy(x_hbm.at[0], xv, lsem.at[1]),
        "og": pltpu.make_async_copy(og_hbm.at[0], og, lsem.at[2]),
    }
    for i, (lo, hi) in enumerate(SPANS):
        loads[lo] = pltpu.make_async_copy(w_hbm.at[:, lo:hi], wv.at[:, lo:hi], lsem.at[3 + i])
    for name in ("x", 1024, "clip"):
        loads[name].start()
    for peer in peers:
        pl.semaphore_signal(barrier, inc=1, device_id=peer, device_id_type=MESH)

    links = Links(send, recv)
    norm = Small(p, links, ns, False)
    dnorm = Small(p, links, ds_, True)
    state = Big(p, links, bs, ssem, False)
    grad = Big(p, links, bg, gsem, True)

    def project(lo, hi):
        r = tn(wv[:, lo:hi], xv[...])
        pos = min(max(2 * HD - lo, 0), hi - lo)
        if pos:
            feat[lo : lo + pos, :] = jnp.maximum(r[:pos], 0.0).astype(BF16)
        if pos < hi - lo:
            feat[lo + pos : hi, :] = r[pos:].astype(BF16)

    for b in (state, grad):
        b.clear()
    loads["clip"].wait()
    is1 = clipv[...] > 0
    m1 = clipv[...].astype(F32)
    m0 = 1.0 - m1
    m0b, m1b = m0.astype(BF16), m1.astype(BF16)

    def split(v, gap=0):
        parts = [v * m0b, v * m1b]
        if gap:
            zero = jnp.zeros((gap, TOK), BF16)
            parts = [parts[0], zero, parts[1], zero]
        return jnp.concatenate(parts, axis=0)

    def put_rows(ref, r):
        ref[...] = jnp.zeros_like(ref)
        for t in range(TILES):
            width = min(WIDE, HD - t * WIDE)
            ref[2 * t : 2 * t + 2, :width] = r[0:2, t * WIDE : t * WIDE + width]

    def get_rows(ref):
        return jnp.concatenate([ref[2 * t : 2 * t + 2, :] for t in range(TILES)], axis=1)

    def columns(ref, dst):
        for t in range(TILES):
            both = ref[2 * t : 2 * t + 2, :]
            both = jnp.concatenate([both, jnp.zeros((6, WIDE), F32)], axis=0)
            dst[t * WIDE : (t + 1) * WIDE, :] = both.T

    def pick(col, h):
        c = col[row_of(h), :]
        return jnp.where(is1, c[:, 1:2], c[:, 0:1])

    def norm_local():
        side = jnp.concatenate([m0b, m1b, jnp.zeros((14, TOK), BF16)], axis=0)
        put_rows(norm.own, nt(side, feat[HD : 2 * HD, :]))

    def put_all(big, terms):
        last = jnp.concatenate([terms(HEADS - 1), jnp.zeros((2 * HEAD, SPARE), F32)], axis=1)
        for h in range(HEADS - 1):
            big.put(h, terms(h), last)

    def state_local():
        put_all(state, lambda h: nt(split(feat[row_of(HEADS + h), :]), feat[row_of(2 * HEADS + h), :]))

    def denominators():
        rows = get_rows(norm.out)[:, :HD]
        keep = in_head(16)
        side = jnp.concatenate(
            [jnp.where(keep, jnp.broadcast_to(rows[c : c + 1], (16, HD)), 0.0) for c in (0, 1)], axis=0
        )
        den = nn(side.astype(BF16), feat[:HD, :])
        inv[...] = 1.0 / (jnp.where(is1, den[16:], den[:16]) + EPS)
        columns(norm.out, ncol)

    def grad_local():
        def terms(h):
            v = (og[row_of(h), :].astype(F32) * inv[h : h + 1, :]).astype(BF16)
            ng[row_of(h), :] = v
            return nt(split(feat[row_of(h), :]), v)

        put_all(grad, terms)

    def attend():
        for h in range(HEADS):
            q = feat[row_of(h), :]
            s0, s1 = state.pair(h)
            r = inv[h : h + 1, :]
            att = tn(jnp.concatenate([s0, s1], axis=0), split(q))[:HEAD] * r
            attv[0, row_of(h), :] = att.astype(BF16)
            d = -jnp.sum(og[row_of(h), :].astype(F32) * att, axis=0, keepdims=True) * r
            dgs[h : h + 1, :] = d
            qg = nn(jnp.concatenate([s0, s1], axis=1), split(ng[row_of(h), :], WIDE - HEAD))
            qg = qg + d * pick(ncol, h)
            grads[row_of(h), :] = jnp.where(q.astype(F32) > 0, qg, 0.0).astype(BF16)

    def dnorm_local():
        d = dgs[...]
        both = jnp.concatenate([d * m0, d * m1], axis=0)
        hi = both.astype(BF16)
        lo = (both - hi.astype(F32)).astype(BF16)
        r = nt(jnp.concatenate([hi, lo], axis=0), feat[:HD, :])
        r = r[:32] + r[32:]
        keep = in_head(16)
        rows = [
            jnp.sum(jnp.where(keep, r[16 * c : 16 * c + 16], 0.0), axis=0, keepdims=True) for c in (0, 1)
        ]
        put_rows(dnorm.own, jnp.concatenate(rows, axis=0))

    def value_grads():
        for h in range(HEADS):
            g0, g1 = grad.pair(h)
            r = tn(jnp.concatenate([g0, g1], axis=0), split(feat[row_of(HEADS + h), :]))
            grads[row_of(2 * HEADS + h), :] = r[:HEAD].astype(BF16)

    def key_grads():
        for h in range(HEADS):
            g0, g1 = grad.pair(h)
            v = feat[row_of(2 * HEADS + h), :]
            kg = nn(jnp.concatenate([g0, g1], axis=1), split(v, WIDE - HEAD)) + pick(dcol, h)
            keep = feat[row_of(HEADS + h), :].astype(F32) > 0
            grads[row_of(HEADS + h), :] = jnp.where(keep, kg, 0.0).astype(BF16)

    def back(lo, hi, kind):
        for m in (0, 1):
            rows = slice(m * HD, (m + 1) * HD)
            r = nn(wv[rows, lo:hi], grads[lo:hi, :])
            if kind > 0:
                r = r + acc[rows, :]
            if kind < 2:
                acc[rows, :] = r
            else:
                outv[0, rows, :] = r.astype(BF16)

    loads["x"].wait()
    loads[1024].wait()
    loads[1408].start()
    loads[2304].start()
    project(1024, 1408)
    loads[1408].wait()
    loads[0].start()
    loads[256].start()
    project(1408, 2304)
    norm_local()
    pl.semaphore_wait(barrier, len(peers))
    norm.s0()
    for peer in p.frame_peers():
        pl.semaphore_signal(entry, inc=1, device_id=peer, device_id_type=MESH)
    loads[2304].wait()
    loads["og"].start()
    project(2304, COLS)
    norm.s1()
    state_local()
    state.s0()
    loads[0].wait()
    project(0, 256)
    pl.semaphore_wait(entry, FRAMES - 1)
    state.s1()
    loads[256].wait()
    project(256, 1024)
    loads["og"].wait()
    norm.s2()
    denominators()
    grad_local()
    grad.s0()
    grad.s1()
    state.s2()
    grad.s2()
    state.s3()
    state.s4()
    attend()
    dnorm_local()
    dnorm.s0()
    back(0, 1024, 0)
    grad.s3()
    dnorm.s1()
    grad.s4()
    value_grads()
    back(2304, COLS, 1)
    dnorm.s2()
    columns(dnorm.out, dcol)
    key_grads()
    back(1024, 2304, 2)
    state.drain()
    grad.drain()
    links.drain()


def per_device(inputs, weight, clip_of_row, out_grad):
    anywhere = pl.BlockSpec(memory_space=pl.ANY)
    att, grad = pl.pallas_call(
        kernel,
        out_shape=(pltpu.VMEM((1, HD, TOK), BF16), pltpu.VMEM((1, D, TOK), BF16)),
        in_specs=[anywhere] * 4,
        out_specs=(pl.BlockSpec(memory_space=pltpu.VMEM),) * 2,
        scratch_shapes=[
            pltpu.VMEM((D, TOK), BF16),
            pltpu.VMEM((D, COLS), BF16),
            pltpu.VMEM((1, TOK), jnp.int32),
            pltpu.VMEM((HD, TOK), BF16),
            pltpu.VMEM((COLS, TOK), BF16),
            pltpu.VMEM((HD, TOK), BF16),
            pltpu.VMEM((16, TOK), F32),
            pltpu.VMEM((16, TOK), F32),
            pltpu.VMEM((COLS, TOK), BF16),
            pltpu.VMEM((D, TOK), F32),
            pltpu.VMEM((TILES * WIDE, 8), F32),
            pltpu.VMEM((TILES * WIDE, 8), F32),
            pltpu.SemaphoreType.DMA((8,)),
            pltpu.SemaphoreType.DMA((COPIES,)),
            pltpu.SemaphoreType.DMA((COPIES,)),
            pltpu.SemaphoreType.DMA((4,)),
            pltpu.SemaphoreType.DMA((4,)),
            pltpu.SemaphoreType.REGULAR,
            *small_scratch(),
            *small_scratch(),
            *big_scratch(),
            *big_scratch(),
        ],
        compiler_params=pltpu.CompilerParams(
            collective_id=0, has_side_effects=True, vmem_limit_bytes=54000000
        ),
    )(inputs.swapaxes(1, 2), weight, clip_of_row, out_grad.swapaxes(1, 2))
    return att.swapaxes(1, 2), grad.swapaxes(1, 2)


def solution(mesh):
    placed = (P("frame", "pack", None), P(), P("frame", "pack"), P("frame", "pack", None))
    return jax.shard_map(
        per_device,
        mesh=mesh,
        in_specs=placed,
        out_specs=(P("frame", "pack", None), P("frame", "pack", None)),
        check_vma=False,
    )
```
